128 devices in a mesh: fx: 8 (over x_lo, z), fy: 16 (over y, x_hi, core).
Axes of the slice: x: 4 (x_hi: 2, x_lo: 2; x = x_hi * 2 + x_lo), y: 4, z: 4, core: 2. Of those that a mesh axis runs over, the one named last changes fastest.
Arguments:
- tracers: float32 [4, 60, 1024, 1024], P(None, None, 'fy', 'fx'), may hold values from -6 to 6
- stream: float32 [60, 1024, 1024], P(None, 'fy', 'fx'), may hold values from -0.45 to 0.45
- land_mask: int32 [1024, 1024], P('fy', 'fx'), may hold values 0 or 1
- convect_mask: int32 [1024, 1024], P('fy', 'fx'), may hold values from 0 to 1, as said below
- regime_label: int32 [1024, 1024], P('fy', 'fx'), may hold values from 0 to 3
- w_in: bfloat16 [512, 241], replicated, may hold values from -0.25 to 0.25
- w_hid: bfloat16 [6, 512, 512], replicated, may hold values from -0.375 to 0.375
- b_hid: float32 [7, 512], replicated, may hold values from -1.5 to 1.5
- w_out: bfloat16 [244, 512], replicated, may hold values from -0.25 to 0.25
- b_out: float32 [244], replicated, may hold values from -2.5 to 2.5
Outputs:
- new_state: float32 [4, 60, 1024, 1024], P(None, None, 'fy', 'fx')
- regime_loss: float32 [1024, 1024], P('fy', 'fx')
The draws below stay inside these ranges and needn't reach their ends.
Inputs may be any that keep to these rules, and one draw needn't show every extreme that they name: `convect_mask`: the face splits into blocks of 64 x 128 cells (one per device). In every strip of blocks that share their cells along the second dimension, exactly one block, drawn at random, holds exactly 4096 active columns and every other block exactly 1024; so every strip holds exactly 19456. Positions within a block are random.
All inputs are finite; a program needn't handle non-finite values. No bound on the sum of `land_mask` on one device may be relied on, other than what follows from the above.
Results may differ from the reference program's by a relative error of at most 0.0026.
Values may be sent and summed in bfloat16 or wider, within the bound.
No kernel may reach another device: no remote copies, remote signals or barrier semaphores. Data moves between devices by JAX's collectives and lax.ppermute only.
A program may use at most 192 MiB of HBM per device.

```python
import jax
import jax.numpy as jnp

CY = 64
CX = 128
LEV = 60
NV = 4
SUBSTEPS = 4
H = 512
NH = 6
K = 4
F_IN = 241
OUTS = 244
CAP = 4096
LOW = 1024
NY = 1024
NX = 1024
N_FX = 8
N_FY = 16


def draw_convect_mask(key, part):
    block = CY * CX
    key_hot = jax.random.fold_in(key, 11)
    key_score = jax.random.fold_in(key, 23)
    hottest = jax.random.randint(key_hot, (1, N_FX, 1), 0, N_FY)
    strips = jnp.arange(N_FY).reshape(N_FY, 1, 1)
    wanted = jnp.where(strips == hottest, CAP, LOW)
    upper = 2 ** 30 // block
    scores = jax.random.randint(key_score, (N_FY, N_FX, block), 0, upper) * block + jnp.arange(block).reshape(1, 1, block)
    ranks = jnp.argsort(jnp.argsort(scores, axis=-1), axis=-1)
    active = (ranks < wanted).astype(jnp.int32)
    return active.reshape(N_FY, N_FX, CY, CX).transpose(0, 2, 1, 3).reshape(NY, NX)


def draw_tracers(key, part):
    key_value = jax.random.fold_in(key, 31)
    rows = jnp.arange(NY) % CY
    cols = jnp.arange(NX) % CX
    row_edge = jnp.minimum(rows, CY - 1 - rows)
    col_edge = jnp.minimum(cols, CX - 1 - cols)
    near = jnp.minimum(row_edge[:, None], col_edge[None, :]) < SUBSTEPS
    weight = jnp.where(near, 1.0, 0.05).astype(jnp.float32)
    rough = jax.random.uniform(key_value, (NV, LEV, NY, NX), jnp.float32, -6.0, 6.0)
    return (rough * weight).astype(jnp.float32)


def draw_stream(key, part):
    key_sign = jax.random.fold_in(key, 41)
    key_size = jax.random.fold_in(key, 43)
    signs = jax.random.rademacher(key_sign, (LEV, NY, NX)).astype(jnp.float32)
    magnitude = jax.random.uniform(key_size, (LEV, NY, NX), jnp.float32, 0.3, 0.45)
    return (signs * magnitude).astype(jnp.float32)


def plant(values, own_key, low, top_value):
    dims = values.shape
    spot = [jax.random.randint(jax.random.fold_in(own_key, axis), (), 0, dims[axis]) for axis in range(len(dims))]
    values = values.at[tuple(spot)].set(low)
    longest = dims.index(max(dims))
    spot[longest] = (spot[longest] + 1) % dims[longest]
    return values.at[tuple(spot)].set(top_value)


def normal_values(rng, dims, spread, most, held_as=jnp.bfloat16):
    return jnp.clip(spread * jax.random.normal(rng, dims, jnp.float32), -most, most).astype(held_as)


def setup_inputs(seed: int = 0) -> dict:
    splits = jax.random.split(jax.random.key(seed), 11)
    return {
        "tracers": draw_tracers(jax.random.fold_in(splits[10], 71), 0),
        "stream": draw_stream(jax.random.fold_in(splits[10], 71), 0),
        "land_mask": plant((jax.random.randint(splits[2], (NY, NX), 0, 10) < 3).astype(jnp.int32), jax.random.fold_in(splits[2], 1), 0, 1),
        "convect_mask": draw_convect_mask(jax.random.fold_in(splits[10], 71), 0),
        "regime_label": plant(jax.random.randint(splits[4], (NY, NX), 0, K), jax.random.fold_in(splits[4], 1), 0, K - 1).astype(jnp.int32),
        "w_in": normal_values(splits[5], (H, F_IN), (2 * F_IN) ** -0.5, 0.25),
        "w_hid": normal_values(splits[6], (NH, H, H), (H // 2) ** -0.5, 0.375),
        "b_hid": normal_values(splits[7], (NH + 1, H), 0.3, 1.5, jnp.float32),
        "w_out": normal_values(splits[8], (OUTS, H), H ** -0.5, 0.25),
        "b_out": normal_values(splits[9], (OUTS,), 0.5, 2.5, jnp.float32),
    }


def face_speeds(padded):
    corner = (padded[:, :-1, :-1] + padded[:, :-1, 1:] + padded[:, 1:, :-1] + padded[:, 1:, 1:]) * 0.25
    east_speed = -(corner[:, 1:, :] - corner[:, :-1, :])
    north_speed = corner[:, :, 1:] - corner[:, :, :-1]
    return east_speed, north_speed


def transport(padded, east_speed, north_speed):
    flux_east = jnp.maximum(east_speed, 0.0) * padded[:, :, 1:-1, :-1] + jnp.minimum(east_speed, 0.0) * padded[:, :, 1:-1, 1:]
    flux_north = jnp.maximum(north_speed, 0.0) * padded[:, :, :-1, 1:-1] + jnp.minimum(north_speed, 0.0) * padded[:, :, 1:, 1:-1]
    centre = padded[:, :, 1:-1, 1:-1]
    return centre - (flux_east[..., 1:] - flux_east[..., :-1]) - (flux_north[:, :, 1:, :] - flux_north[:, :, :-1, :])


def run_network(inputs, w_in, w_hid, b_hid, w_out, b_out):
    hidden = jax.nn.leaky_relu(jnp.dot(w_in, inputs, preferred_element_type=jnp.float32) + b_hid[0][:, None], negative_slope=0.15).astype(jnp.bfloat16)
    for hidden_index in range(w_hid.shape[0]):
        summed = jnp.dot(w_hid[hidden_index], hidden, preferred_element_type=jnp.float32) + b_hid[hidden_index + 1][:, None]
        hidden = jax.nn.leaky_relu(summed, negative_slope=0.15).astype(jnp.bfloat16)
    return (jnp.dot(w_out, hidden, preferred_element_type=jnp.float32) + b_out[:, None]).astype(jnp.bfloat16)


def reference(tracers, stream, land_mask, convect_mask, regime_label, w_in, w_hid, b_hid, w_out, b_out):
    east_speed, north_speed = face_speeds(jnp.pad(stream, ((0, 0), (1, 1), (1, 1))))
    field = tracers
    for substep in range(SUBSTEPS):
        field = transport(jnp.pad(field, ((0, 0), (0, 0), (1, 1), (1, 1))), east_speed, north_speed)
    columns = NY * NX
    flat_state = field.reshape(NV * LEV, columns)
    land_row = 4.0 * land_mask.reshape(1, columns).astype(jnp.float32)
    features = jnp.concatenate([flat_state, land_row], axis=0).astype(jnp.bfloat16)
    flat_active = convect_mask.reshape(columns)
    total = N_FX * (CAP + (N_FY - 1) * LOW)
    chosen = jnp.nonzero(flat_active, size=total, fill_value=0)[0].astype(jnp.int32)
    result = run_network(features[:, chosen], w_in, w_hid, b_hid, w_out, b_out)
    per_cell = jnp.zeros((NV * LEV + K, columns), jnp.bfloat16).at[:, chosen].set(result)
    active = flat_active.astype(jnp.float32)
    tendency = per_cell[:NV * LEV].astype(jnp.float32) * active[None, :]
    new_state = (flat_state + tendency).reshape(NV, LEV, NY, NX)
    evidence = per_cell[NV * LEV:].astype(jnp.float32)
    alpha = 1.0 + jax.nn.softplus(evidence)
    strength = jnp.sum(alpha, axis=0)
    labels = regime_label.reshape(1, columns)
    picked = jnp.sum(jnp.where(labels == jnp.arange(K).reshape(K, 1), alpha, 0.0), axis=0)
    loss = active * (jnp.log(strength) - jnp.log(picked))
    return new_state, loss.reshape(NY, NX)
```

```python
import functools

import jax
import jax.numpy as jnp
from jax import lax
from jax.experimental import pallas as pl
from jax.experimental.pallas import tpu as pltpu
from jax.sharding import PartitionSpec as P

F32, BF16, I32 = jnp.float32, jnp.bfloat16, jnp.int32
SUBSTEPS = 4
NV, LEV, LT = 4, 60, 8
ROWS, COLS = 64, 128
SLOTS = NV * 64
HALO_ROWS = SLOTS + 64
NT = (((1,), (1,)), ((), ()))
TILE = 1024
CAP = 4096
VMEM_LIMIT = 60 << 20


def lanes():
    return lax.broadcasted_iota(I32, (8, COLS), 1)


def gather_edges(vals, lane):
    out = vals[0]
    where = ((lane + 16) & 127) >> 5
    for f in range(1, NV):
        out = jnp.where(where == f, pltpu.roll(vals[f], 32 * f, 1), out)
    return out


def speed_coefs(above, here, below):
    diff = above - below
    east = 0.25 * (pltpu.roll(diff, 1, 1) + diff)
    east_next = pltpu.roll(east, COLS - 1, 1)
    top, bottom = above + here, here + below
    north = 0.25 * (pltpu.roll(top, COLS - 1, 1) - pltpu.roll(top, 1, 1))
    south = 0.25 * (pltpu.roll(bottom, COLS - 1, 1) - pltpu.roll(bottom, 1, 1))
    w, e = jnp.maximum(east, 0.0), jnp.maximum(-east_next, 0.0)
    n, s = jnp.maximum(north, 0.0), jnp.maximum(-south, 0.0)
    return w, e, n, s, 1.0 - ((w + e) + (n + s))


def update(c, up, cell, down):
    w, e, n, s, keep = c
    return (
        (keep * cell + w * pltpu.roll(cell, 1, 1))
        + (e * pltpu.roll(cell, COLS - 1, 1) + n * up)
        + s * down
    )


def edges_kernel(x_hbm, s_hbm, left, right, top, bottom, c_tl, c_tr, c_bl, c_br, xv, sv, sem):
    def copies(g):
        return (
            pltpu.make_async_copy(
                x_hbm.at[:, pl.ds(g * 8, 8), :], xv.at[g, pl.ds(0, NV * LEV)], sem.at[0, g]
            ),
            pltpu.make_async_copy(
                s_hbm.at[:, pl.ds(g * 8, 8), :], sv.at[g, pl.ds(0, LEV)], sem.at[1, g]
            ),
        )

    for g in range(8):
        for c in copies(g):
            c.start()
    lane = lanes()
    slot = (lane & 31) >> 2
    xr = xv.reshape(8, (NV * LEV + 4) * 8, COLS)
    sr = sv.reshape(8, 64 * 8, COLS)

    def tracer(g, r, f, lt):
        return xr[g, pl.ds((f * LEV + lt * 8) * 8 + r, 8, stride=8), :]

    def flow(g, r, lt):
        return sr[g, pl.ds(lt * 64 + r, 8, stride=8), :]

    @pl.loop(0, 8)
    def _(g):
        for c in copies(g):
            c.wait()
        for pair in range(4):
            packed = []
            for r in (2 * pair, 2 * pair + 1):
                tl = tr = sl = s_r = None
                for lt in range(LT):
                    e = gather_edges([tracer(g, r, f, lt) for f in range(NV)], lane)
                    v = flow(g, r, lt)
                    es = gather_edges([v] * NV, lane)
                    a, b = pltpu.roll(e, 4 * lt, 1) if lt else e, pltpu.roll(e, 4 * lt + 4, 1)
                    p, q = pltpu.roll(es, 4 * lt, 1) if lt else es, pltpu.roll(es, 4 * lt + 4, 1)
                    if lt == 0:
                        tl, tr, sl, s_r = a, b, p, q
                    else:
                        here = slot == lt
                        tl, tr = jnp.where(here, a, tl), jnp.where(here, b, tr)
                        sl, s_r = jnp.where(here, p, sl), jnp.where(here, q, s_r)
                packed.append((tl, tr, sl, s_r))
            tl, tr, sl, s_r = [
                jnp.concatenate([packed[0][i], packed[1][i]], axis=0).astype(BF16) for i in range(4)
            ]
            at = pl.multiple_of(g * 64 + pair * 16, 16)
            left[pl.ds(at, 16), :] = tl
            left[pl.ds(512 + at, 16), :] = sl
            right[pl.ds(at, 16), :] = tr
            right[pl.ds(512 + at, 16), :] = s_r
    c_tl[pl.ds(0, 32), :] = left[pl.ds(0, 32), :]
    c_tl[pl.ds(32, 32), :] = left[pl.ds(512, 32), :]
    c_bl[pl.ds(0, 32), :] = left[pl.ds(480, 32), :]
    c_bl[pl.ds(32, 32), :] = left[pl.ds(992, 32), :]
    c_tr[pl.ds(0, 32), :] = right[pl.ds(0, 32), :]
    c_tr[pl.ds(32, 32), :] = right[pl.ds(512, 32), :]
    c_br[pl.ds(0, 32), :] = right[pl.ds(480, 32), :]
    c_br[pl.ds(32, 32), :] = right[pl.ds(992, 32), :]
    for ref, g, r0 in ((top, 0, 0), (bottom, 7, 4)):
        for r in range(4):
            for f in range(NV):
                for lt in range(0, LT, 2):
                    two = [tracer(g, r0 + r, f, lt), tracer(g, r0 + r, f, lt + 1)]
                    ref[pl.ds(r * HALO_ROWS + f * 64 + lt * 8, 16), :] = jnp.concatenate(
                        two, axis=0
                    ).astype(BF16)
            for lt in range(0, LT, 2):
                two = [flow(g, r0 + r, lt), flow(g, r0 + r, lt + 1)]
                ref[pl.ds(r * HALO_ROWS + SLOTS + lt * 8, 16), :] = jnp.concatenate(
                    two, axis=0
                ).astype(BF16)


def edges_call(x3, s3):
    side = jax.ShapeDtypeStruct((1024, COLS), BF16)
    row = jax.ShapeDtypeStruct((4 * HALO_ROWS, COLS), BF16)
    corner = jax.ShapeDtypeStruct((64, COLS), BF16)
    return pl.pallas_call(
        edges_kernel,
        name="edges",
        out_shape=(side, side, row, row, corner, corner, corner, corner),
        in_specs=[pl.BlockSpec(memory_space=pl.ANY)] * 2,
        out_specs=[pl.BlockSpec(memory_space=pltpu.VMEM)] * 8,
        scratch_shapes=[
            pltpu.VMEM((8, NV * LEV + 4, 8, COLS), F32),
            pltpu.VMEM((8, 64, 8, COLS), F32),
            pltpu.SemaphoreType.DMA((2, 8)),
        ],
        compiler_params=pltpu.CompilerParams(vmem_limit_bytes=VMEM_LIMIT),
    )(x3, s3)


def interior_kernel(x_ref, s_ref, m_ref, state, strips, local, base, cf, buf):
    lane = lanes()

    @pl.when(pl.program_id(0) == 0)
    def _():
        mask = m_ref[...]
        m = mask.astype(F32).astype(BF16)
        before = (
            lax.broadcasted_iota(I32, (COLS, COLS), 0) < lax.broadcasted_iota(I32, (COLS, COLS), 1)
        )
        before = jnp.where(before, 1.0, 0.0).astype(BF16)
        inside = jnp.dot(m, before, preferred_element_type=F32).astype(I32)
        local[...] = jnp.where(mask == 1, inside, -(1 << 20))
        counts = lax.dot_general(jnp.ones((8, COLS), BF16), m, NT, preferred_element_type=F32)
        base[...] = jnp.dot(
            counts.astype(BF16), before[:ROWS, :], preferred_element_type=F32
        ).astype(I32)

    @pl.loop(0, ROWS // 8)
    def _(block):
        r0 = block * 8
        flows = {}
        for r in range(-1, 9):
            at = jnp.clip(r0 + r, 0, ROWS - 1) if r in (-1, 8) else r0 + r
            flows[r] = s_ref[pl.ds(at, 8, stride=ROWS), :]
        for r in range(8):
            c = speed_coefs(flows[r - 1], flows[r], flows[r + 1])
            for i in range(5):
                cf[i, r0 + r] = c[i]
            vals = [x_ref[f, pl.ds(r0 + r, 8, stride=ROWS), :] for f in range(NV)]
            for f in range(NV):
                buf[0, f, r0 + r] = vals[f]
            e = gather_edges(vals, lane)
            strips[0, r0 + r] = jnp.where((lane & 31) < 8, e, pltpu.roll(e, 24, 1))

    def sweep(read, write):
        span = 32

        @pl.loop(0, ROWS // span)
        def _(block):
            r0 = block * span
            ups = [read(f, jnp.maximum(r0 - 1, 0)) for f in range(NV)]
            cells = [read(f, r0) for f in range(NV)]
            for r in range(span):
                c = [cf[i, r0 + r] for i in range(5)]
                at = jnp.minimum(r0 + r + 1, ROWS - 1) if r == span - 1 else r0 + r + 1
                for f in range(NV):
                    down = read(f, at)
                    write(f, r0 + r, update(c, ups[f], cells[f], down))
                    ups[f], cells[f] = cells[f], down

    @pl.loop(0, SUBSTEPS - 1)
    def _(step):
        src = step & 1

        def write(f, r, v):
            buf[1 - src, f, r] = v

        sweep(lambda f, r: buf[src, f, r], write)

    last = (SUBSTEPS - 1) & 1

    def write_out(f, r, v):
        state[r, f, 0] = v

    sweep(lambda f, r: buf[last, f, r], write_out)


def interior_call(tracers, stream, mask):
    return pl.pallas_call(
        interior_kernel,
        name="interior",
        grid=(LT,),
        out_shape=(
            jax.ShapeDtypeStruct((ROWS, NV, LT, 8, COLS), F32),
            jax.ShapeDtypeStruct((LT, ROWS, 8, COLS), F32),
            jax.ShapeDtypeStruct((ROWS, COLS), I32),
            jax.ShapeDtypeStruct((8, COLS), I32),
        ),
        in_specs=[
            pl.BlockSpec((NV, 8 * ROWS, COLS), lambda i: (0, i, 0)),
            pl.BlockSpec((8 * ROWS, COLS), lambda i: (i, 0)),
            pl.BlockSpec((ROWS, COLS), lambda i: (0, 0)),
        ],
        out_specs=(
            pl.BlockSpec((ROWS, NV, 1, 8, COLS), lambda i: (0, 0, i, 0, 0)),
            pl.BlockSpec((1, ROWS, 8, COLS), lambda i: (i, 0, 0, 0)),
            pl.BlockSpec((ROWS, COLS), lambda i: (0, 0)),
            pl.BlockSpec((8, COLS), lambda i: (0, 0)),
        ),
        scratch_shapes=[
            pltpu.VMEM((5, ROWS, 8, COLS), F32),
            pltpu.VMEM((2, NV, ROWS, 8, COLS), F32),
        ],
        compiler_params=pltpu.CompilerParams(
            dimension_semantics=("arbitrary",), vmem_limit_bytes=VMEM_LIMIT
        ),
        cost_estimate=pl.CostEstimate(
            flops=2_000_000_000, bytes_accessed=20_000_000, transcendentals=0
        ),
    )(tracers.reshape(NV, LEV * ROWS, COLS), stream.reshape(LEV * ROWS, COLS), mask)


def leaky(v):
    return jnp.maximum(v, 0.15 * v).astype(BF16)


def finish_kernel(
    place,
    base,
    h_left,
    h_right,
    h_top,
    h_bottom,
    c_tl,
    c_tr,
    c_bl,
    c_br,
    local,
    land,
    mask,
    label,
    bh_ref,
    bo_ref,
    x_hbm,
    s_hbm,
    state_hbm,
    strips_hbm,
    w_in_hbm,
    w_hid_hbm,
    w_out_hbm,
    out_hbm,
    loss,
    sv,
    strips,
    xr,
    sr,
    hf,
    rf,
    g,
    cf,
    packed,
    result,
    w_in,
    w_hid,
    w_out,
    w_in_p,
    w_out_p,
    bias,
    ov,
    ev,
    sem,
    osem,
):
    weights = [
        pltpu.make_async_copy(w_in_hbm, w_in, sem.at[0]),
        pltpu.make_async_copy(w_hid_hbm, w_hid, sem.at[1]),
        pltpu.make_async_copy(w_out_hbm, w_out, sem.at[2]),
    ]
    fields = [
        pltpu.make_async_copy(
            x_hbm.at[:, pl.ds(0, 8), :], xr.at[0, pl.ds(0, NV * LEV)], sem.at[3]
        ),
        pltpu.make_async_copy(
            x_hbm.at[:, pl.ds(ROWS - 8, 8), :], xr.at[1, pl.ds(0, NV * LEV)], sem.at[4]
        ),
        pltpu.make_async_copy(s_hbm, sr.at[pl.ds(0, LEV)], sem.at[5]),
    ]
    bulk = [
        pltpu.make_async_copy(state_hbm, sv, sem.at[6]),
        pltpu.make_async_copy(strips_hbm, strips, sem.at[7]),
    ]
    for c in fields + bulk + weights:
        c.start()

    lane = lanes()
    slot = (lane & 31) >> 2
    first_row, last_row = place[0] == 0, place[0] == place[2] - 1
    first_col, last_col = place[1] == 0, place[1] == place[3] - 1

    for half in range(2):
        for side, (ref, up, down) in enumerate(((h_left, c_tl, c_bl), (h_right, c_tr, c_br))):
            at = (half * 2 + side) * 576
            hf[pl.ds(at, 32), :] = up[pl.ds(half * 32, 32), :].astype(F32)
            hf[pl.ds(at + 544, 32), :] = down[pl.ds(half * 32, 32), :].astype(F32)

            @pl.loop(0, 4)
            def _(i):
                hf[pl.ds(at + 32 + i * 128, 128), :] = ref[
                    pl.ds(pl.multiple_of(half * 512 + i * 128, 128), 128), :
                ].astype(F32)

    for side, ref in enumerate((h_top, h_bottom)):

        @pl.loop(0, 4)
        def _(i):
            rf[pl.ds(side * 4 * HALO_ROWS + i * HALO_ROWS, HALO_ROWS), :] = ref[
                pl.ds(pl.multiple_of(i * HALO_ROWS, 64), HALO_ROWS), :
            ].astype(F32)

    packed[...] = jnp.zeros_like(packed)
    for c in fields:
        c.wait()
    for c in bulk:
        c.wait()
    xr2 = xr.reshape(2, (NV * LEV + 4) * 8, COLS)
    sr2 = sr.reshape(64 * ROWS, COLS)

    def flow(r, lt):
        return sr2[pl.ds(lt * 8 * ROWS + r, 8, stride=ROWS), :]

    def halo_row(side, r, at):
        return rf[pl.ds(pl.multiple_of((side * 4 + r) * HALO_ROWS + at, 8), 8), :]

    @pl.loop(0, LT)
    def _(lt):
        for side in range(2):
            if side == 0:
                flows = [halo_row(0, r, SLOTS + lt * 8) for r in range(4)]
                flows += [flow(r, lt) for r in range(8)]
                outside = lambda r: r < 4
                closed = first_row
            else:
                flows = [flow(ROWS - 8 + r, lt) for r in range(8)]
                flows += [halo_row(1, r, SLOTS + lt * 8) for r in range(4)]
                outside = lambda r: r >= 8
                closed = last_row
            for r in range(1, 11):
                c = speed_coefs(flows[r - 1], flows[r], flows[r + 1])
                for i in range(5):
                    cf[i, r] = jnp.where(closed, 0.0, c[i]) if outside(r) else c[i]
            for f in range(NV):
                own = [
                    xr2[side, pl.ds((f * LEV + lt * 8) * 8 + r, 8, stride=8), :] for r in range(8)
                ]
                halo = [halo_row(side, r, f * 64 + lt * 8) for r in range(4)]
                rows = halo + own if side == 0 else own + halo
                for step in range(SUBSTEPS):
                    lo, hi = step + 1, 10 - step
                    new = list(rows)
                    for r in range(lo, hi + 1):
                        c = [cf[i, r] for i in range(5)]
                        new[r] = update(c, rows[r - 1], rows[r], rows[r + 1])
                    rows = new
                for r in range(4):
                    target = r if side == 0 else ROWS - 4 + r
                    sv[target, pl.ds(pl.multiple_of(f * 64 + lt * 8, 8), 8), :] = rows[4 + r]

    west_out = jnp.logical_and(first_col, slot == 7)
    east_out = jnp.logical_and(last_col, slot == 6)
    closed_lane = jnp.logical_or(west_out, east_out)
    closed_f = jnp.where(closed_lane, 0.0, 1.0)

    @pl.loop(0, LT)
    def _(lt):
        to_east = (24 - 4 * lt) & 127
        to_west = (124 - 4 * lt) & 127

        def with_halo(own, half, r):
            lefts = hf[pl.ds(pl.multiple_of((half * 2) * 576 + r * 8, 8), 8), :]
            rights = hf[pl.ds(pl.multiple_of((half * 2 + 1) * 576 + r * 8, 8), 8), :]
            v = jnp.where(slot == 6, pltpu.roll(rights, to_east, 1), own)
            return jnp.where(slot == 7, pltpu.roll(lefts, to_west, 1), v)

        def spread(vals):
            e = gather_edges(vals, lane)
            return jnp.where((lane & 31) < 8, e, pltpu.roll(e, 24, 1))

        for side in range(2):
            for r in range(4):
                row = r if side == 0 else 68 + r
                vals = [halo_row(side, r, f * 64 + lt * 8) for f in range(NV)]
                g[0, row] = with_halo(spread(vals), 0, row)
                v = halo_row(side, r, SLOTS + lt * 8)
                g[2, row] = with_halo(spread([v] * NV), 1, row)

        @pl.loop(0, 8)
        def _(block):
            for k in range(8):
                r = block * 8 + k
                g[0, r + 4] = with_halo(strips[lt, r], 0, r + 4)
                v = flow(r, lt)
                g[2, r + 4] = with_halo(spread([v] * NV), 1, r + 4)

        @pl.loop(0, 7)
        def _(block):
            r0 = block * 10 + 1
            flows = [g[2, r0 + k] for k in range(-1, 11)]
            for k in range(10):
                r = r0 + k
                c = speed_coefs(flows[k], flows[k + 1], flows[k + 2])
                out_row = jnp.logical_or(
                    jnp.logical_and(first_row, r < 4), jnp.logical_and(last_row, r >= 68)
                )
                keep = jnp.where(out_row, 0.0, closed_f)
                for i in range(5):
                    cf[i, r] = c[i] * keep

        for step in range(SUBSTEPS):
            src = step & 1
            for part in range(2):
                r0, r1 = (step + 1, 36) if part == 0 else (36, 71 - step)
                up, cell = g[src, r0 - 1], g[src, r0]
                for r in range(r0, r1):
                    down = g[src, r + 1]
                    g[1 - src, r] = update([cf[i, r] for i in range(5)], up, cell, down)
                    up, cell = cell, down

        @pl.loop(0, 8)
        def _(block):
            for k in range(8):
                r = block * 8 + k
                v = g[0, r + 4]
                for f in range(NV):
                    at = pl.ds(pl.multiple_of(f * 64 + lt * 8, 8), 8)
                    west = pltpu.roll(v, (128 - 32 * f) & 127, 1) if f else v
                    east = pltpu.roll(v, (104 - 32 * f) & 127, 1)
                    old = sv[r, at, :]
                    sv[r, at, :] = jnp.where(lane < 4, west, jnp.where(lane >= 124, east, old))

    for c in weights:
        c.wait()
    slot_id = lax.broadcasted_iota(I32, (256, 256), 0)
    source = lax.broadcasted_iota(I32, (256, 256), 1)
    level = slot_id & 63
    wanted = jnp.where(level < LEV, (slot_id >> 6) * LEV + level, -1)
    for_in = jnp.where(slot_id == LEV, NV * LEV, wanted)
    for_out = jnp.where(
        jnp.logical_and(slot_id >= LEV, slot_id < 64), NV * LEV + slot_id - LEV, wanted
    )
    pick_in = jnp.where(for_in == source, 1.0, 0.0).astype(BF16)
    pick_out = jnp.where(for_out == source, 1.0, 0.0).astype(BF16)
    n_in, n_out = w_in.shape[1], w_out.shape[0]
    w_in_p[...] = lax.dot_general(
        w_in[...], pick_in[:, :n_in], NT, preferred_element_type=F32
    ).astype(BF16)
    w_out_p[...] = jnp.dot(pick_out[:, :n_out], w_out[...], preferred_element_type=F32).astype(BF16)
    flat = jnp.concatenate([bh_ref[...], jnp.zeros((120, 512), F32)], axis=0)
    bias[...] = jnp.transpose(flat)
    out_bias = jnp.sum(
        jnp.where(for_out == source, jnp.broadcast_to(bo_ref[0:1, :], (256, 256)), 0.0),
        axis=1,
        keepdims=True,
    )

    spot = lax.broadcasted_iota(I32, (256, COLS), 0)
    real = (lax.broadcasted_iota(I32, (256, COLS), 0) & 63) < LEV
    land_slot = lax.broadcasted_iota(I32, (256, COLS), 0) == LEV

    def one_hot(r):
        offset = base[r] & 127
        return jnp.where(spot == local[pl.ds(r, 1), :] + offset, 1.0, 0.0).astype(BF16)

    def window(r):
        return pl.ds(pl.multiple_of((base[r] >> 7) * 128, 128), 256)

    @pl.loop(0, ROWS)
    def _(r):
        land_row = 4.0 * land[pl.ds(r, 1), :].astype(F32)
        x = jnp.where(real, sv[r], jnp.where(land_slot, land_row, 0.0)).astype(BF16)
        moved = lax.dot_general(x, one_hot(r), NT, preferred_element_type=F32).astype(BF16)
        packed[:, window(r)] += moved

    count = base[ROWS]
    tiles = (count + TILE - 1) // TILE

    @pl.loop(0, tiles)
    def _(i):
        half = TILE // 2
        hs = []
        for c in range(2):
            at = pl.ds(pl.multiple_of(i * TILE + c * half, half), half)
            hs.append(
                leaky(
                    jnp.dot(w_in_p[...], packed[:, at], preferred_element_type=F32) + bias[:, 0:1]
                )
            )
        for layer in range(6):
            for c in range(2):
                hs[c] = leaky(
                    jnp.dot(w_hid[layer], hs[c], preferred_element_type=F32)
                    + bias[:, layer + 1 : layer + 2]
                )
        for c in range(2):
            at = pl.ds(pl.multiple_of(i * TILE + c * half, half), half)
            result[:, at] = (
                jnp.dot(w_out_p[...], hs[c], preferred_element_type=F32) + out_bias
            ).astype(BF16)

    result[:, pl.ds(pl.multiple_of(tiles * TILE, TILE), 256)] = jnp.zeros((256, 256), BF16)

    ov2 = ov.reshape(8, (NV * LEV + 4) * 8, COLS)

    def out_copy(block):
        return pltpu.make_async_copy(
            ov.at[block, pl.ds(0, NV * LEV)],
            out_hbm.at[:, pl.ds(block * 8, 8), :],
            osem.at[block],
        )

    @pl.loop(0, ROWS // 8)
    def _(block):
        @pl.loop(0, 8)
        def _(k):
            r = block * 8 + k
            back = jnp.dot(result[:, window(r)], one_hot(r), preferred_element_type=F32)
            for i in range(K_REGIMES):
                ev[i, pl.ds(r, 1), :] = back[LEV + i : LEV + i + 1, :]
            new = sv[r] + back
            for f in range(NV):
                for lt in range(LT):
                    at = f * 64 + lt * 8
                    ov2[block, pl.ds((f * LEV + lt * 8) * 8 + k, 8, stride=8), :] = new[at : at + 8]

        out_copy(block).start()

    alphas = [1.0 + jax.nn.softplus(ev[i]) for i in range(K_REGIMES)]
    total = (alphas[0] + alphas[1]) + (alphas[2] + alphas[3])
    picked = jnp.zeros_like(total)
    for i in range(K_REGIMES):
        picked = jnp.where(label[...] == i, alphas[i], picked)
    loss[...] = jnp.where(mask[...] == 1, jnp.log(total) - jnp.log(picked), 0.0)
    for block in range(8):
        out_copy(block).wait()


K_REGIMES = 4


def finish_call(place, base, halos, local, land, mask, label, bh, bo, x3, s3, state, strips, ws):
    w_in, w_hid, w_out = ws
    smem = pl.BlockSpec(memory_space=pltpu.SMEM)
    vmem = pl.BlockSpec(memory_space=pltpu.VMEM)
    anyw = pl.BlockSpec(memory_space=pl.ANY)
    return pl.pallas_call(
        finish_kernel,
        name="finish",
        out_shape=(
            jax.ShapeDtypeStruct((NV * LEV, ROWS, COLS), F32),
            jax.ShapeDtypeStruct((ROWS, COLS), F32),
        ),
        in_specs=[smem, smem] + [vmem] * 14 + [anyw] * 7,
        out_specs=(anyw, vmem),
        scratch_shapes=[
            pltpu.VMEM((ROWS, SLOTS, COLS), F32),
            pltpu.VMEM((LT, ROWS, 8, COLS), F32),
            pltpu.VMEM((2, NV * LEV + 4, 8, COLS), F32),
            pltpu.VMEM((64, ROWS, COLS), F32),
            pltpu.VMEM((4 * 576, COLS), F32),
            pltpu.VMEM((8 * HALO_ROWS, COLS), F32),
            pltpu.VMEM((3, 72, 8, COLS), F32),
            pltpu.VMEM((5, 72, 8, COLS), F32),
            pltpu.VMEM((256, CAP + 256), BF16),
            pltpu.VMEM((256, CAP + 256), BF16),
            pltpu.VMEM(w_in.shape, BF16),
            pltpu.VMEM(w_hid.shape, BF16),
            pltpu.VMEM(w_out.shape, BF16),
            pltpu.VMEM((512, 256), BF16),
            pltpu.VMEM((256, 512), BF16),
            pltpu.VMEM((512, 128), F32),
            pltpu.VMEM((8, NV * LEV + 4, 8, COLS), F32),
            pltpu.VMEM((K_REGIMES, ROWS, COLS), F32),
            pltpu.SemaphoreType.DMA((8,)),
            pltpu.SemaphoreType.DMA((8,)),
        ],
        compiler_params=pltpu.CompilerParams(vmem_limit_bytes=VMEM_LIMIT),
    )(
        place, base, *halos, local, land, mask, label, bh, bo, x3, s3, state, strips, w_in, w_hid,
        w_out,
    )


def body(tracers, stream, land_mask, convect_mask, regime_label, w_in, w_hid, b_hid, w_out, b_out):
    x3 = tracers.reshape(NV * LEV, ROWS, COLS)
    left, right, top, bottom, c_tl, c_tr, c_bl, c_br = edges_call(x3, stream)
    ny, nx = lax.axis_size("fy"), lax.axis_size("fx")
    j, i = lax.axis_index("fy"), lax.axis_index("fx")

    def move(v, dj, di):
        pairs = [
            (b * ny + a, (b + di) * ny + a + dj)
            for a in range(ny)
            for b in range(nx)
            if 0 <= a + dj < ny and 0 <= b + di < nx
        ]
        return lax.ppermute(v, ("fx", "fy"), pairs)

    halos = (
        move(right, 0, 1),
        move(left, 0, -1),
        move(bottom, 1, 0),
        move(top, -1, 0),
        move(c_br, 1, 1),
        move(c_bl, 1, -1),
        move(c_tr, -1, 1),
        move(c_tl, -1, -1),
    )
    state, strips, local, base = interior_call(tracers, stream, convect_mask)
    place = jnp.stack([j, i, jnp.int32(ny), jnp.int32(nx)]).astype(I32)
    bh = jnp.pad(b_hid, ((0, 1), (0, 0)))
    bo = jnp.pad(b_out.reshape(1, -1), ((0, 7), (0, 256 - b_out.shape[0])))
    new_state, loss = finish_call(
        place,
        base[0],
        halos,
        local,
        land_mask,
        convect_mask,
        regime_label,
        bh,
        bo,
        x3,
        stream,
        state.reshape(ROWS, SLOTS, COLS),
        strips,
        (w_in, w_hid, w_out),
    )
    return new_state.reshape(tracers.shape), loss


def solution(mesh):
    placed = (
        P(None, None, "fy", "fx"),
        P(None, "fy", "fx"),
        P("fy", "fx"),
        P("fy", "fx"),
        P("fy", "fx"),
        P(),
        P(),
        P(),
        P(),
        P(),
    )
    return jax.shard_map(
        body,
        mesh=mesh,
        in_specs=placed,
        out_specs=(P(None, None, "fy", "fx"), P("fy", "fx")),
        check_vma=False,
    )
```

```python
import jax
import jax.numpy as jnp
from jax import lax
from jax.experimental import pallas as pl
from jax.experimental.pallas import tpu as pltpu
from jax.sharding import PartitionSpec as P

F32, BF16, I32 = jnp.float32, jnp.bfloat16, jnp.int32
SUBSTEPS = 4
NV, LEV, LT = 4, 60, 8
ROWS, COLS = 64, 128
SLOTS = NV * 64
HALO_ROWS = SLOTS + 64
NT = (((1,), (1,)), ((), ()))
TILE = 1024
CAP = 4096
K_REGIMES = 4
EXT = ROWS + 8
VMEM_LIMIT = 61 << 20


def iota(shape, dim):
    return lax.broadcasted_iota(I32, shape, dim)


def ones_where(cond):
    return jnp.where(cond, 1.0, 0.0).astype(BF16)


def split(x):
    high = x.astype(BF16)
    low = (x - high.astype(F32)).astype(BF16)
    return jnp.concatenate([high, low], axis=1)


def shift_matrix():
    k, c = iota((256, 256), 0) & 127, iota((256, 256), 1)
    west = jnp.logical_and(c < COLS, ((k + 1) & 127) == c)
    east = jnp.logical_and(c >= COLS, ((k - 1) & 127) == c - COLS)
    return ones_where(jnp.logical_or(west, east))


def strip_matrix(f):
    k, c = iota((256, COLS), 0) & 127, iota((256, COLS), 1)
    own = jnp.logical_or(
        jnp.logical_and(k < 8, c == 32 * f + k),
        jnp.logical_and(k >= COLS - 8, c == 32 * f + k - (COLS - 24)),
    )
    return ones_where(own)


def strip_of(rows, mats):
    out = None
    for x, m in zip(rows, mats):
        part = jnp.dot(x, m, preferred_element_type=F32)
        out = part if out is None else out + part
    return out


def edges_kernel(
    x_hbm,
    s_hbm,
    m_ref,
    left,
    right,
    top,
    bottom,
    c_tl,
    c_tr,
    c_bl,
    c_br,
    local,
    base,
    strips_hbm,
    flow_strips_hbm,
    xv,
    sv,
    st,
    fst,
    pick,
    sem,
    osem,
):
    def copies(r):
        return (
            pltpu.make_async_copy(
                x_hbm.at[:, :, r, :], xv.at[r, :, pl.ds(0, LEV), :], sem.at[0, r]
            ),
            pltpu.make_async_copy(s_hbm.at[:, r, :], sv.at[r, pl.ds(0, LEV), :], sem.at[1, r]),
        )

    @pl.loop(0, ROWS)
    def _(r):
        for c in copies(r):
            c.start()

    for f in range(NV):
        pick[f] = strip_matrix(f)
    pick[NV] = (pick[0] + pick[1]) + (pick[2] + pick[3])
    mask = m_ref[...]
    m = mask.astype(F32).astype(BF16)
    before = ones_where(iota((COLS, COLS), 0) < iota((COLS, COLS), 1))
    inside = jnp.dot(m, before, preferred_element_type=F32).astype(I32)
    local[...] = jnp.where(mask == 1, inside, -(1 << 20))
    counts = lax.dot_general(jnp.ones((8, COLS), BF16), m, NT, preferred_element_type=F32)
    base[...] = jnp.dot(
        counts.astype(BF16), before[:ROWS, :], preferred_element_type=F32
    ).astype(I32)

    @pl.loop(0, ROWS // 2)
    def _(pair):
        for k in range(2):
            r = pair * 2 + k
            for c in copies(r):
                c.wait()
        for k in range(2):
            r = pair * 2 + k
            st[r] = strip_of([split(xv[r, f]) for f in range(NV)], [pick[f] for f in range(NV)])
            fst[r] = strip_of([split(sv[r])], [pick[NV]])

    outs = [
        pltpu.make_async_copy(st, strips_hbm, osem.at[0]),
        pltpu.make_async_copy(fst, flow_strips_hbm, osem.at[1]),
    ]
    for c in outs:
        c.start()
    k, c = iota((COLS, 256), 0), iota((COLS, 256), 1)
    q = k & 31
    for half, ref in enumerate((st, fst)):
        for part in range(2):
            total = None
            for lt in range(LT):
                to_left = jnp.logical_and(q < 4, c == k + 4 * lt)
                to_right = jnp.logical_and(
                    jnp.logical_and(q >= 20, q < 24), c == COLS + k - 20 + 4 * lt
                )
                place = ones_where(jnp.logical_or(to_left, to_right))
                x = ref[pl.ds(part * 32, 32), pl.ds(lt * 8, 8), :].reshape(256, COLS).astype(BF16)
                y = jnp.dot(x, place, preferred_element_type=F32)
                total = y if total is None else total + y
            at = pl.ds(half * 512 + part * 256, 256)
            left[at, :] = total[:, :COLS].astype(BF16)
            right[at, :] = total[:, COLS:].astype(BF16)
    for half in range(2):
        dst = pl.ds(32 * half, 32)
        c_tl[dst, :] = left[pl.ds(512 * half, 32), :]
        c_bl[dst, :] = left[pl.ds(512 * half + 480, 32), :]
        c_tr[dst, :] = right[pl.ds(512 * half, 32), :]
        c_br[dst, :] = right[pl.ds(512 * half + 480, 32), :]
    for ref, r0 in ((top, 0), (bottom, ROWS - 4)):
        for r in range(4):
            for f in range(NV):
                ref[pl.ds(r * HALO_ROWS + f * 64, 64), :] = xv[r0 + r, f].astype(BF16)
            ref[pl.ds(r * HALO_ROWS + SLOTS, 64), :] = sv[r0 + r].astype(BF16)
    for c in outs:
        c.wait()


def edges_call(tracers, stream, mask):
    side = jax.ShapeDtypeStruct((1024, COLS), BF16)
    row = jax.ShapeDtypeStruct((4 * HALO_ROWS, COLS), BF16)
    corner = jax.ShapeDtypeStruct((64, COLS), BF16)
    strips = jax.ShapeDtypeStruct((ROWS, 64, COLS), F32)
    vmem, anyw = pl.BlockSpec(memory_space=pltpu.VMEM), pl.BlockSpec(memory_space=pl.ANY)
    return pl.pallas_call(
        edges_kernel,
        name="edges",
        out_shape=(side, side, row, row, corner, corner, corner, corner)
        + (jax.ShapeDtypeStruct((ROWS, COLS), I32), jax.ShapeDtypeStruct((8, COLS), I32))
        + (strips, strips),
        in_specs=[anyw, anyw, vmem],
        out_specs=[vmem] * 10 + [anyw] * 2,
        scratch_shapes=[
            pltpu.VMEM((ROWS, NV, 64, COLS), F32),
            pltpu.VMEM((ROWS, 64, COLS), F32),
            pltpu.VMEM((ROWS, 64, COLS), F32),
            pltpu.VMEM((ROWS, 64, COLS), F32),
            pltpu.VMEM((NV + 1, 256, COLS), BF16),
            pltpu.SemaphoreType.DMA((2, ROWS)),
            pltpu.SemaphoreType.DMA((2,)),
        ],
        compiler_params=pltpu.CompilerParams(vmem_limit_bytes=VMEM_LIMIT),
    )(tracers, stream, mask)


def leaky(v):
    return jnp.maximum(v, 0.15 * v).astype(BF16)


def finish_kernel(
    base,
    h_left,
    h_right,
    h_top,
    h_bottom,
    c_tl,
    c_tr,
    c_bl,
    c_br,
    local,
    land,
    mask,
    label,
    bh_ref,
    bo_ref,
    x_hbm,
    s_hbm,
    strips_hbm,
    flow_strips_hbm,
    w_in_hbm,
    w_hid_hbm,
    w_out_hbm,
    out_hbm,
    loss,
    field,
    flows,
    side,
    shifted,
    coef,
    g,
    hcat,
    pick,
    shift,
    back_pick,
    packed,
    result,
    w_in,
    w_hid,
    w_out,
    w_in_p,
    w_out_p,
    bias,
    flat,
    ev,
    sem,
    rsem,
    osem,
):
    def row_copies(r):
        return (
            pltpu.make_async_copy(
                x_hbm.at[:, :, r, :], field.at[0, r + 4, :, pl.ds(0, LEV), :], rsem.at[0, r]
            ),
            pltpu.make_async_copy(
                s_hbm.at[:, r, :], flows.at[r + 4, pl.ds(0, LEV), :], rsem.at[1, r]
            ),
        )

    @pl.loop(0, ROWS)
    def _(r):
        for c in row_copies(r):
            c.start()

    strip_copies = [
        pltpu.make_async_copy(strips_hbm, g.at[0, pl.ds(4, ROWS)], sem.at[3]),
        pltpu.make_async_copy(flow_strips_hbm, side.at[pl.ds(4, ROWS)], sem.at[4]),
    ]
    weights = [
        pltpu.make_async_copy(w_in_hbm, w_in, sem.at[0]),
        pltpu.make_async_copy(w_hid_hbm, w_hid, sem.at[1]),
        pltpu.make_async_copy(w_out_hbm, w_out, sem.at[2]),
    ]
    for c in strip_copies + weights:
        c.start()

    first_row = lax.axis_index("fy") == 0
    last_row = lax.axis_index("fy") == lax.axis_size("fy") - 1
    first_col = lax.axis_index("fx") == 0
    last_col = lax.axis_index("fx") == lax.axis_size("fx") - 1

    for f in range(NV):
        pick[f] = strip_matrix(f)
    pick[NV] = (pick[0] + pick[1]) + (pick[2] + pick[3])
    shift[...] = shift_matrix()
    k, c = iota((256, 512), 0) & 127, iota((256, 512), 1)
    f, cell = c >> 7, c & 127
    back_pick[...] = ones_where(
        jnp.logical_or(
            jnp.logical_and(cell < 4, k == 32 * f + cell),
            jnp.logical_and(cell >= COLS - 4, k == 32 * f + cell - (COLS - 24)),
        )
    )
    packed[...] = jnp.zeros_like(packed)

    for ref, r0 in ((h_top, 0), (h_bottom, EXT - 4)):
        for r in range(4):
            xs = [ref[pl.ds(r * HALO_ROWS + f * 64, 64), :] for f in range(NV)]
            v = ref[pl.ds(r * HALO_ROWS + SLOTS, 64), :]
            for f in range(NV):
                field[0, r0 + r, f] = xs[f].astype(F32)
            flows[r0 + r] = v.astype(F32)
            g[0, r0 + r] = strip_of(xs, [pick[f, pl.ds(0, COLS), :] for f in range(NV)])
            side[r0 + r] = strip_of([v], [pick[NV, pl.ds(0, COLS), :]])
    for half in range(2):
        for s, (ref, up, down) in enumerate(((h_left, c_tl, c_bl), (h_right, c_tr, c_br))):
            at = pl.ds(s * COLS, COLS)
            hcat[half, pl.ds(0, 32), at] = up[pl.ds(half * 32, 32), :]
            hcat[half, pl.ds(32, 512), at] = ref[pl.ds(half * 512, 512), :]
            hcat[half, pl.ds(544, 32), at] = down[pl.ds(half * 32, 32), :]

    lane1 = iota((1, COLS), 1)
    slot = (lane1 & 31) >> 2
    closed_lane = jnp.logical_or(
        jnp.logical_and(first_col, slot == 7), jnp.logical_and(last_col, slot == 6)
    )
    lane_open = jnp.where(closed_lane, 0.0, 1.0)

    def make_coefs(rows, open_lanes):
        @pl.loop(0, EXT // 4)
        def _(block):
            x = rows[pl.ds(block * 4, 4)].reshape(256, COLS)
            y = jnp.dot(split(x), shift[...], preferred_element_type=F32)
            shifted[0, pl.ds(block * 4, 4)] = y[:, :COLS].reshape(4, 64, COLS)
            shifted[1, pl.ds(block * 4, 4)] = y[:, COLS:].reshape(4, 64, COLS)

        @pl.loop(0, 35)
        def _(block):
            for i in range(2):
                r = block * 2 + 1 + i
                up, down = rows[r - 1], rows[r + 1]
                up_w, here_w, down_w = shifted[0, r - 1], shifted[0, r], shifted[0, r + 1]
                up_e, here_e, down_e = shifted[1, r - 1], shifted[1, r], shifted[1, r + 1]
                diff = up - down
                east = 0.25 * (diff + (up_w - down_w))
                east_next = 0.25 * (diff + (up_e - down_e))
                here = here_e - here_w
                north = 0.25 * ((up_e - up_w) + here)
                south = 0.25 * (here + (down_e - down_w))
                closed = jnp.logical_or(
                    jnp.logical_and(first_row, r < 4), jnp.logical_and(last_row, r >= EXT - 4)
                )
                keep = jnp.where(closed, 0.0, 1.0)
                if open_lanes is not None:
                    keep = keep * open_lanes
                w, e = jnp.maximum(east, 0.0), jnp.maximum(-east_next, 0.0)
                n, s = jnp.maximum(north, 0.0), jnp.maximum(-south, 0.0)
                stay = 1.0 - ((w + e) + (n + s))
                for j, v in enumerate((w, e, n, s, stay)):
                    coef[j, r] = v * keep

    @pl.loop(0, ROWS)
    def _(r):
        for c in row_copies(r):
            c.wait()

    make_coefs(flows, None)
    for step in range(SUBSTEPS):
        src, dst = step & 1, 1 - (step & 1)

        @pl.loop(0, (EXT - 2) // 2 - step)
        def _(block):
            for i in range(2):
                r = step + 1 + block * 2 + i
                cell = field[src, r]
                y = jnp.dot(
                    split(cell.reshape(256, COLS)), shift[...], preferred_element_type=F32
                )
                w, e, n, s, stay = (coef[j, r][None] for j in range(5))
                west = y[:, :COLS].reshape(NV, 64, COLS)
                east = y[:, COLS:].reshape(NV, 64, COLS)
                field[dst, r] = ((stay * cell + w * west) + (e * east + n * field[src, r - 1])) + (
                    s * field[src, r + 1]
                )

    for c in strip_copies:
        c.wait()
    k, c = iota((256, COLS), 0), iota((256, COLS), 1)
    for half, ref in enumerate((g.at[0], side)):
        for lt in range(LT):
            mine = ((k & 31) >> 2) == lt
            target = jnp.where(k < COLS, k - 4 * lt - 4, k - 4 * lt + 24) & 127
            u = ones_where(jnp.logical_and(mine, c == target))
            for part in range(2):
                y = jnp.dot(hcat[half, pl.ds(part * 288, 288), :], u, preferred_element_type=F32)
                at = (pl.ds(part * 36, 36), pl.ds(lt * 8, 8))
                ref[at[0], at[1], :] = ref[at[0], at[1], :] + y.reshape(36, 8, COLS)
    make_coefs(side, lane_open)
    for step in range(SUBSTEPS):
        src, dst = step & 1, 1 - (step & 1)
        total = EXT - 2 - 2 * step

        def strip_rows(r, count):
            cell = g[src, pl.ds(r, count)].reshape(count * 64, COLS)
            y = jnp.dot(split(cell), shift[...], preferred_element_type=F32)
            up = g[src, pl.ds(r - 1, count)].reshape(count * 64, COLS)
            down = g[src, pl.ds(r + 1, count)].reshape(count * 64, COLS)
            w, e, n, s, stay = (
                coef[j, pl.ds(r, count)].reshape(count * 64, COLS) for j in range(5)
            )
            new = ((stay * cell + w * y[:, :COLS]) + (e * y[:, COLS:] + n * up)) + s * down
            g[dst, pl.ds(r, count)] = new.reshape(count, 64, COLS)

        @pl.loop(0, total // 4)
        def _(block):
            strip_rows(step + 1 + block * 4, 4)

        if total % 4:
            strip_rows(step + 1 + total - 2, 2)

    for c in weights:
        c.wait()
    slot_id, source = iota((256, 256), 0), iota((256, 256), 1)
    level = slot_id & 63
    wanted = jnp.where(level < LEV, (slot_id >> 6) * LEV + level, -1)
    for_in = jnp.where(slot_id == LEV, NV * LEV, wanted)
    for_out = jnp.where(
        jnp.logical_and(slot_id >= LEV, slot_id < 64), NV * LEV + slot_id - LEV, wanted
    )
    pick_in, pick_out = ones_where(for_in == source), ones_where(for_out == source)
    n_in, n_out = w_in.shape[0], w_out.shape[0]
    w_in_t = jnp.dot(pick_in[:, :n_in], w_in[...], preferred_element_type=F32).astype(BF16)
    eye = ones_where(iota((512, 512), 0) == iota((512, 512), 1))
    w_in_p[...] = lax.dot_general(eye, w_in_t, NT, preferred_element_type=F32).astype(BF16)
    w_out_p[...] = jnp.dot(pick_out[:, :n_out], w_out[...], preferred_element_type=F32).astype(BF16)
    flat[...] = jnp.zeros_like(flat)
    flat[0:7, :] = bh_ref[...]
    flat[8:9, 0:n_out] = bo_ref[...]
    out_row = jnp.broadcast_to(flat[8:9, 0:256], (256, 256))
    out_bias = jnp.sum(jnp.where(for_out == source, out_row, 0.0), axis=1, keepdims=True)
    bias[...] = jnp.transpose(flat[...])

    spot = iota((256, COLS), 0)
    real = (iota((256, COLS), 0) & 63) < LEV
    land_slot = iota((256, COLS), 0) == LEV
    edge_lane = jnp.logical_or(iota((64, COLS), 1) < 4, iota((64, COLS), 1) >= COLS - 4)

    def one_hot(r):
        offset = base[0, r] & 127
        return ones_where(spot == local[pl.ds(r, 1), :] + offset)

    def window(r):
        return pl.ds(pl.multiple_of((base[0, r] >> 7) * 128, 128), 256)

    @pl.loop(0, ROWS)
    def _(r):
        edge = jnp.dot(split(g[0, r + 4]), back_pick[...], preferred_element_type=F32)
        for f in range(NV):
            field[0, r + 4, f] = jnp.where(
                edge_lane, edge[:, f * COLS : (f + 1) * COLS], field[0, r + 4, f]
            )
        land_row = 4.0 * land[pl.ds(r, 1), :].astype(F32)
        state = field[0, r + 4].reshape(256, COLS)
        x = jnp.where(real, state, jnp.where(land_slot, land_row, 0.0)).astype(BF16)
        moved = lax.dot_general(x, one_hot(r), NT, preferred_element_type=F32).astype(BF16)
        packed[:, window(r)] += moved

    tiles = (base[0, ROWS] + TILE - 1) // TILE

    @pl.loop(0, tiles)
    def _(i):
        half = TILE // 2
        hs = []
        for c in range(2):
            at = pl.ds(pl.multiple_of(i * TILE + c * half, half), half)
            hs.append(
                leaky(
                    jnp.dot(w_in_p[...], packed[:, at], preferred_element_type=F32) + bias[:, 0:1]
                )
            )
        for layer in range(6):
            for c in range(2):
                hs[c] = leaky(
                    jnp.dot(w_hid[layer], hs[c], preferred_element_type=F32)
                    + bias[:, layer + 1 : layer + 2]
                )
        for c in range(2):
            at = pl.ds(pl.multiple_of(i * TILE + c * half, half), half)
            result[:, at] = (
                jnp.dot(w_out_p[...], hs[c], preferred_element_type=F32) + out_bias
            ).astype(BF16)

    result[:, pl.ds(pl.multiple_of(tiles * TILE, TILE), 256)] = jnp.zeros((256, 256), BF16)

    def out_copy(r):
        return pltpu.make_async_copy(
            field.at[1, r + 4, :, pl.ds(0, LEV), :], out_hbm.at[:, :, r, :], osem.at[r]
        )

    @pl.loop(0, ROWS)
    def _(r):
        back = jnp.dot(result[:, window(r)], one_hot(r), preferred_element_type=F32)
        for i in range(K_REGIMES):
            ev[i, pl.ds(r, 1), :] = back[LEV + i : LEV + i + 1, :]
        field[1, r + 4] = field[0, r + 4] + back.reshape(NV, 64, COLS)
        out_copy(r).start()

    alphas = [1.0 + jax.nn.softplus(ev[i]) for i in range(K_REGIMES)]
    total = (alphas[0] + alphas[1]) + (alphas[2] + alphas[3])
    picked = jnp.zeros_like(total)
    for i in range(K_REGIMES):
        picked = jnp.where(label[...] == i, alphas[i], picked)
    loss[...] = jnp.where(mask[...] == 1, jnp.log(total) - jnp.log(picked), 0.0)

    @pl.loop(0, ROWS)
    def _(r):
        out_copy(r).wait()


def finish_call(base, halos, local, land, mask, label, bh, bo, tracers, stream, strips, fst, ws):
    w_in, w_hid, w_out = ws
    smem = pl.BlockSpec(memory_space=pltpu.SMEM)
    vmem = pl.BlockSpec(memory_space=pltpu.VMEM)
    anyw = pl.BlockSpec(memory_space=pl.ANY)
    return pl.pallas_call(
        finish_kernel,
        name="finish",
        out_shape=(
            jax.ShapeDtypeStruct(tracers.shape, F32),
            jax.ShapeDtypeStruct((ROWS, COLS), F32),
        ),
        in_specs=[smem] + [vmem] * 14 + [anyw] * 7,
        out_specs=(anyw, vmem),
        scratch_shapes=[
            pltpu.VMEM((2, EXT, NV, 64, COLS), F32),
            pltpu.VMEM((EXT, 64, COLS), F32),
            pltpu.VMEM((EXT, 64, COLS), F32),
            pltpu.VMEM((2, EXT, 64, COLS), F32),
            pltpu.VMEM((5, EXT, 64, COLS), F32),
            pltpu.VMEM((2, EXT, 64, COLS), F32),
            pltpu.VMEM((2, EXT * 8, 256), BF16),
            pltpu.VMEM((NV + 1, 256, COLS), BF16),
            pltpu.VMEM((256, 256), BF16),
            pltpu.VMEM((256, 512), BF16),
            pltpu.VMEM((256, CAP + 256), BF16),
            pltpu.VMEM((256, CAP + 256), BF16),
            pltpu.VMEM(w_in.shape, BF16),
            pltpu.VMEM(w_hid.shape, BF16),
            pltpu.VMEM(w_out.shape, BF16),
            pltpu.VMEM((512, 256), BF16),
            pltpu.VMEM((256, 512), BF16),
            pltpu.VMEM((512, 128), F32),
            pltpu.VMEM((128, 512), F32),
            pltpu.VMEM((K_REGIMES, ROWS, COLS), F32),
            pltpu.SemaphoreType.DMA((5,)),
            pltpu.SemaphoreType.DMA((2, ROWS)),
            pltpu.SemaphoreType.DMA((ROWS,)),
        ],
        compiler_params=pltpu.CompilerParams(vmem_limit_bytes=VMEM_LIMIT),
    )(
        base, *halos, local, land, mask, label, bh, bo, tracers, stream, strips, fst, w_in, w_hid,
        w_out,
    )


def body(tracers, stream, land_mask, convect_mask, regime_label, w_in, w_hid, b_hid, w_out, b_out):
    (left, right, top, bottom, c_tl, c_tr, c_bl, c_br, local, base, strips, flow_strips) = (
        edges_call(tracers, stream, convect_mask)
    )
    ny, nx = lax.axis_size("fy"), lax.axis_size("fx")

    def move(v, dj, di):
        pairs = [
            (b * ny + a, (b + di) * ny + a + dj)
            for a in range(ny)
            for b in range(nx)
            if 0 <= a + dj < ny and 0 <= b + di < nx
        ]
        return lax.ppermute(v, ("fx", "fy"), pairs)

    halos = (
        move(right, 0, 1),
        move(left, 0, -1),
        move(bottom, 1, 0),
        move(top, -1, 0),
        move(c_br, 1, 1),
        move(c_bl, 1, -1),
        move(c_tr, -1, 1),
        move(c_tl, -1, -1),
    )
    return finish_call(
        base,
        halos,
        local,
        land_mask,
        convect_mask,
        regime_label,
        b_hid,
        b_out.reshape(1, -1),
        tracers,
        stream,
        strips,
        flow_strips,
        (w_in.T, w_hid, w_out),
    )


def solution(mesh):
    placed = (
        P(None, None, "fy", "fx"),
        P(None, "fy", "fx"),
        P("fy", "fx"),
        P("fy", "fx"),
        P("fy", "fx"),
        P(),
        P(),
        P(),
        P(),
        P(),
    )
    return jax.shard_map(
        body,
        mesh=mesh,
        in_specs=placed,
        out_specs=(P(None, None, "fy", "fx"), P("fy", "fx")),
        check_vma=False,
    )
```

```python
import jax
import jax.numpy as jnp
from jax import lax
from jax.experimental import pallas as pl
from jax.experimental.pallas import tpu as pltpu
from jax.sharding import PartitionSpec as P

F32, BF16, I32 = jnp.float32, jnp.bfloat16, jnp.int32
SUBSTEPS = 4
NV, LEV = 4, 60
ROWS, COLS = 64, 128
SLOTS = NV * 64
HALO_ROWS = SLOTS + 64
EXT = ROWS + 8
STRIDE = COLS + 16
CELLS = EXT * STRIDE
SPARE = COLS
SIDE = EXT * 4 + 16
NT = (((1,), (1,)), ((), ()))
TILE = 1024
CAP = 4096
WINDOW = COLS + 16
K_REGIMES = 4
VMEM_LIMIT = 61 << 20


def iota(shape, dim):
    return lax.broadcasted_iota(I32, shape, dim)


def ones_where(cond):
    return jnp.where(cond, 1.0, 0.0).astype(BF16)


def edges_kernel(x_hbm, s_hbm, m_ref, left, right, top, bottom, local, base, xv, sv, sem):
    def copies(r):
        return (
            pltpu.make_async_copy(
                x_hbm.at[:, :, r, :], xv.at[r, :, pl.ds(0, LEV), :], sem.at[0, r // 8]
            ),
            pltpu.make_async_copy(
                s_hbm.at[:, r, :], sv.at[r, pl.ds(0, LEV), :], sem.at[1, r // 8]
            ),
        )

    def landed(group):
        x = xv.at[pl.ds(group * 8, 8), :, pl.ds(0, LEV), :]
        v = sv.at[pl.ds(group * 8, 8), pl.ds(0, LEV), :]
        return (
            pltpu.make_async_copy(x, x, sem.at[0, group]),
            pltpu.make_async_copy(v, v, sem.at[1, group]),
        )

    @pl.loop(0, ROWS)
    def _(r):
        for c in copies(r):
            c.start()

    mask = m_ref[...]
    m = mask.astype(F32).astype(BF16)
    before = ones_where(iota((COLS, COLS), 0) < iota((COLS, COLS), 1))
    inside = jnp.dot(m, before, preferred_element_type=F32).astype(I32)
    local[...] = jnp.where(mask == 1, inside, -(1 << 20))
    counts = lax.dot_general(jnp.ones((8, COLS), BF16), m, NT, preferred_element_type=F32)
    base[...] = jnp.dot(
        counts.astype(BF16), before[:ROWS, :], preferred_element_type=F32
    ).astype(I32)

    out, k = iota((16, 256), 0), iota((16, 256), 1)
    q, odd, far = out & 3, (out >> 2) & 1, out >> 3
    pick = ones_where(k == odd * COLS + far * (COLS - 4) + q)

    @pl.loop(0, ROWS // 8)
    def _(group):
        for c in landed(group):
            c.wait()
        for half in range(2):
            sides = []
            for pair in range(2):
                r = group * 8 + half * 4 + pair * 2
                x = [xv[r + i].reshape(256, COLS).astype(BF16) for i in range(2)]
                v = [jnp.concatenate([sv[r + i], sv[r + i]], axis=0).astype(BF16) for i in range(2)]
                y = lax.dot_general(
                    pick, jnp.concatenate(x, axis=1), NT, preferred_element_type=F32
                )
                z = lax.dot_general(
                    pick, jnp.concatenate(v, axis=1), NT, preferred_element_type=F32
                )
                sides.append((y[:, :COLS], y[:, COLS:], z))
            at = pl.multiple_of(group * 32 + half * 16, 16)
            for part in range(3):
                for i, ref in enumerate((left, right)):
                    two = [sides[pair][part][8 * i : 8 * i + 8] for pair in range(2)]
                    ref[pl.ds(part * 256 + at, 16), :] = jnp.concatenate(two, axis=0).astype(BF16)

    for ref, r0 in ((top, 0), (bottom, ROWS - 4)):
        for r in range(4):
            for f in range(NV):
                ref[pl.ds(r * HALO_ROWS + f * 64, 64), :] = xv[r0 + r, f].astype(BF16)
            ref[pl.ds(r * HALO_ROWS + SLOTS, 64), :] = sv[r0 + r].astype(BF16)


def edges_call(tracers, stream, mask):
    side = jax.ShapeDtypeStruct((3 * 256, COLS), BF16)
    row = jax.ShapeDtypeStruct((4 * HALO_ROWS, COLS), BF16)
    vmem, anyw = pl.BlockSpec(memory_space=pltpu.VMEM), pl.BlockSpec(memory_space=pl.ANY)
    return pl.pallas_call(
        edges_kernel,
        name="edges",
        out_shape=(side, side, row, row)
        + (jax.ShapeDtypeStruct((ROWS, COLS), I32), jax.ShapeDtypeStruct((8, COLS), I32)),
        in_specs=[anyw, anyw, vmem],
        out_specs=[vmem] * 6,
        scratch_shapes=[
            pltpu.VMEM((ROWS, NV, 64, COLS), F32),
            pltpu.VMEM((ROWS, 64, COLS), F32),
            pltpu.SemaphoreType.DMA((2, ROWS // 8)),
        ],
        compiler_params=pltpu.CompilerParams(vmem_limit_bytes=VMEM_LIMIT),
    )(tracers, stream, mask)


def leaky(v):
    return jnp.maximum(v, 0.15 * v).astype(BF16)


def finish_kernel(
    base,
    h_left,
    h_right,
    h_top,
    h_bottom,
    local,
    land,
    mask,
    label,
    bh_ref,
    bo_ref,
    x_hbm,
    s_hbm,
    w_in_hbm,
    w_hid_hbm,
    w_out_hbm,
    out_hbm,
    loss,
    a0,
    a1,
    b0,
    b1,
    coef,
    side,
    packed,
    result,
    w_in,
    w_hid,
    w_out,
    w_in_p,
    w_out_p,
    bo_pad,
    ev,
    sem,
    rsem,
    osem,
):
    field = ((a0, a1), (b0, b1))
    stage = [b.reshape((CELLS + SPARE) // 128, 2, 64, COLS) for b in (b0, b1)]
    flow_stage = coef.reshape(5 * CELLS // 64, 64, COLS)

    def row_copies(r, i):
        if i == 2:
            src, dst = s_hbm.at[:, r, :], flow_stage.at[r, pl.ds(0, LEV), :]
        else:
            src, dst = x_hbm.at[pl.ds(2 * i, 2), :, r, :], stage[i].at[r, :, pl.ds(0, LEV), :]
        return pltpu.make_async_copy(src, dst, rsem.at[i, r // 8])

    @pl.loop(0, ROWS)
    def _(r):
        row_copies(r, 2).start()

    @pl.loop(0, ROWS)
    def _(r):
        for h in range(2):
            row_copies(r, h).start()

    weights = [
        pltpu.make_async_copy(w_in_hbm, w_in, sem.at[0]),
        pltpu.make_async_copy(w_hid_hbm, w_hid, sem.at[1]),
        pltpu.make_async_copy(w_out_hbm, w_out, sem.at[2]),
    ]
    for c in weights:
        c.start()

    first_row = lax.axis_index("fy") == 0
    last_row = lax.axis_index("fy") == lax.axis_size("fy") - 1
    first_col = lax.axis_index("fx") == 0
    last_col = lax.axis_index("fx") == lax.axis_size("fx") - 1

    packed[...] = jnp.zeros_like(packed)

    def cells_of(r):
        return pl.ds(pl.multiple_of(r * STRIDE + 8, 8), COLS)

    for part in range(3):
        for i, ref in enumerate((h_left, h_right)):
            corner = pl.ds(4 * HALO_ROWS + i * 48 + part * 16, 16)
            at = (part * 2 + i) * SIDE + 8
            side[pl.ds(at, 16), :] = h_top[corner, :].astype(F32)
            side[pl.ds(at + 16, 256), :] = ref[pl.ds(part * 256, 256), :].astype(F32)
            side[pl.ds(at + 272, 16), :] = h_bottom[corner, :].astype(F32)

    def beside(part, ref, offset, scale):
        @pl.loop(0, EXT // 8)
        def _(group):
            for k in range(8):
                r = group * 8 + k
                at = pl.multiple_of(r * STRIDE + offset, 8)
                west = side[pl.ds(part * 2 * SIDE + 4 + r * 4, 8), :]
                east = side[pl.ds((part * 2 + 1) * SIDE + 8 + r * 4, 8), :]
                ref[pl.ds(at, 8), :] = west if scale is None else scale * west
                ref[pl.ds(at + 8 + COLS, 8), :] = east if scale is None else scale * east

    for ref, r0 in ((h_top, 0), (h_bottom, EXT - 4)):
        for r in range(4):
            v = 0.25 * ref[pl.ds(r * HALO_ROWS + SLOTS, 64), :].astype(F32)
            a0[pl.ds((r0 + r) * STRIDE + 16, COLS), :] = jnp.transpose(
                jnp.concatenate([v, v], axis=0)
            )

    @pl.loop(0, ROWS // 8)
    def _(group):
        v = flow_stage.at[pl.ds(group * 8, 8), pl.ds(0, LEV), :]
        pltpu.make_async_copy(v, v, rsem.at[2, group]).wait()
        for k in range(8):
            r = group * 8 + k
            v = 0.25 * flow_stage[r]
            at = pl.multiple_of((r + 4) * STRIDE + 16, 8)
            a0[pl.ds(at, COLS), :] = jnp.transpose(jnp.concatenate([v, v], axis=0))

    beside(2, a0, 8, 0.25)

    @pl.loop(0, 2)
    def _(block):
        @pl.loop(0, STRIDE // 8)
        def _(tile):
            q0 = pl.multiple_of((block * 35 + 1) * STRIDE + tile * 8, 8)

            def row(t):
                here = q0 + (t * STRIDE + 8)
                w, c, e = (a0[pl.ds(here + i, 8), :] for i in (-1, 0, 1))
                return w, c, e, e - w

            up, here = row(-1), row(0)
            for t in range(35):
                down = row(t + 1)
                diff = up[1] - down[1]
                w = jnp.maximum(diff + (up[0] - down[0]), 0.0)
                e = jnp.maximum((down[2] - up[2]) - diff, 0.0)
                n = jnp.maximum(up[3] + here[3], 0.0)
                s = jnp.maximum(-(here[3] + down[3]), 0.0)
                stay = 1.0 - ((w + e) + (n + s))
                for j, v in enumerate((w, e, n, s, stay)):
                    coef[j, pl.ds(q0 + t * STRIDE, 8), :] = v
                up, here = here, down

    def close_rows(r0):
        for j in range(5):
            coef[j, pl.ds(r0 * STRIDE, 3 * STRIDE), :] = jnp.zeros((3 * STRIDE, COLS), F32)

    def close_cols(offset):
        @pl.loop(1, EXT - 1)
        def _(r):
            for j in range(5):
                coef[j, pl.ds(pl.multiple_of(r * STRIDE + offset, 8), 8), :] = jnp.zeros(
                    (8, COLS), F32
                )

    pl.when(first_row)(lambda: close_rows(1))
    pl.when(last_row)(lambda: close_rows(EXT - 4))
    pl.when(first_col)(lambda: close_cols(0))
    pl.when(last_col)(lambda: close_cols(8 + COLS))

    for ref, r0 in ((h_top, 0), (h_bottom, EXT - 4)):
        for r in range(4):
            for h in range(2):
                x = ref[pl.ds(r * HALO_ROWS + h * 128, 128), :].astype(F32)
                field[0][h][pl.ds((r0 + r) * STRIDE + 8, COLS), :] = jnp.transpose(x)

    @pl.loop(0, ROWS // 8)
    def _(group):
        rows = pl.ds(group * 8, 8)
        for h in range(2):
            x = stage[h].at[rows, :, pl.ds(0, LEV), :]
            pltpu.make_async_copy(x, x, rsem.at[h, group]).wait()
        for k in range(8):
            r = group * 8 + k
            for h in range(2):
                x = stage[h][r].reshape(128, COLS)
                field[0][h][cells_of(r + 4), :] = jnp.transpose(x)

    for h in range(2):
        beside(h, field[0][h], 0, None)

    for step in range(SUBSTEPS):
        src, dst = field[step & 1], field[1 - (step & 1)]
        span = (EXT - 2 - 2 * step) // 2
        skip = 1 if step == SUBSTEPS - 1 else 0

        @pl.loop(0, 2)
        def _(block):
            @pl.loop(skip, STRIDE // 8 - skip)
            def _(tile):
                q0 = pl.multiple_of((block * span + step + 1) * STRIDE + tile * 8, 8)

                def at(h, t, offset=0):
                    return src[h][pl.ds(q0 + (t * STRIDE + offset), 8), :]

                up = [at(h, -1) for h in range(2)]
                cell = [at(h, 0) for h in range(2)]
                for t in range(span):
                    q = q0 + t * STRIDE
                    w, e, n, s, stay = (coef[j, pl.ds(q, 8), :] for j in range(5))
                    for h in range(2):
                        down = at(h, t + 1)
                        own = stay * cell[h] + w * at(h, t, -1)
                        ahead = e * at(h, t, 1) + n * up[h]
                        dst[h][pl.ds(q, 8), :] = (own + ahead) + s * down
                        up[h], cell[h] = cell[h], down

    for c in weights:
        c.wait()
    slot_id, source = iota((256, 256), 0), iota((256, 256), 1)
    level = slot_id & 63
    wanted = jnp.where(level < LEV, (slot_id >> 6) * LEV + level, -1)
    for_in = jnp.where(slot_id == LEV, NV * LEV, wanted)
    for_out = jnp.where(
        jnp.logical_and(slot_id >= LEV, slot_id < 64), NV * LEV + slot_id - LEV, wanted
    )
    pick_in, pick_out = ones_where(for_in == source), ones_where(for_out == source)
    n_in, n_out = w_in.shape[0], w_out.shape[0]
    w_in_p[...] = jnp.dot(pick_in[:, :n_in], w_in[...], preferred_element_type=F32).astype(BF16)
    w_out_p[...] = jnp.dot(pick_out[:, :n_out], w_out[...], preferred_element_type=F32).astype(BF16)
    bo_pad[...] = jnp.zeros_like(bo_pad)
    bo_pad[0:1, 0:n_out] = bo_ref[...]
    out_row = jnp.broadcast_to(bo_pad[0:1, :], (256, 256))
    out_bias = jnp.sum(jnp.where(for_out == source, out_row, 0.0), axis=1, keepdims=True)

    real = (iota((COLS, 256), 1) & 63) < LEV
    land_slot = jnp.where(iota((COLS, 256), 1) == LEV, 4.0, 0.0).astype(BF16)
    window_spot = iota((WINDOW, COLS), 0)
    spot = iota((256, COLS), 0)

    @pl.loop(0, ROWS // 2)
    def _(pair):
        moved = []
        for k in range(2):
            r = pair * 2 + k
            x = jnp.concatenate(
                [field[0][h][cells_of(r + 4), :] for h in range(2)], axis=1
            )
            x = jnp.where(real, x, 0.0).astype(BF16)
            hit = window_spot == local[pl.ds(r, 1), :] + (base[0, r] & 15)
            land_hit = jnp.logical_and(hit, land[pl.ds(r, 1), :] == 1)
            hot = jnp.concatenate([ones_where(hit), ones_where(land_hit)], axis=1)
            moved.append(
                jnp.dot(
                    hot, jnp.concatenate([x, land_slot], axis=0), preferred_element_type=F32
                ).astype(BF16)
            )
        for k in range(2):
            r = pair * 2 + k
            packed[pl.ds(pl.multiple_of((base[0, r] >> 4) * 16, 16), WINDOW), :] += moved[k]

    tiles = (base[0, ROWS] + TILE - 1) // TILE

    @pl.loop(0, tiles)
    def _(i):
        half = TILE // 2
        hs = []
        for c in range(2):
            at = pl.ds(pl.multiple_of(i * TILE + c * half, half), half)
            hs.append(
                leaky(
                    jnp.dot(packed[at, :], w_in_p[...], preferred_element_type=F32)
                    + bh_ref[0:1, :]
                )
            )
        for layer in range(6):
            for c in range(2):
                hs[c] = leaky(
                    lax.dot_general(hs[c], w_hid[layer], NT, preferred_element_type=F32)
                    + bh_ref[layer + 1 : layer + 2, :]
                )
        for c in range(2):
            at = pl.ds(pl.multiple_of(i * TILE + c * half, half), half)
            result[:, at] = (
                lax.dot_general(w_out_p[...], hs[c], NT, preferred_element_type=F32) + out_bias
            ).astype(BF16)

    result[:, pl.ds(pl.multiple_of(tiles * TILE, TILE), 256)] = jnp.zeros((256, 256), BF16)

    def out_copies(r):
        return [
            pltpu.make_async_copy(
                stage[h].at[r, :, pl.ds(0, LEV), :],
                out_hbm.at[pl.ds(2 * h, 2), :, r, :],
                osem.at[h, r // 8],
            )
            for h in range(2)
        ]

    @pl.loop(0, ROWS // 4)
    def _(block):
        for k in range(4):
            r = block * 4 + k
            hot = ones_where(spot == local[pl.ds(r, 1), :] + (base[0, r] & 127))
            at = pl.ds(pl.multiple_of((base[0, r] >> 7) * 128, 128), 256)
            back = jnp.dot(result[:, at], hot, preferred_element_type=F32)
            for i in range(K_REGIMES):
                ev[i, pl.ds(r, 1), :] = back[LEV + i : LEV + i + 1, :]
            for h in range(2):
                new = jnp.transpose(field[0][h][cells_of(r + 4), :]) + back[h * 128 : h * 128 + 128]
                stage[h][r] = new.reshape(2, 64, COLS)
        for k in range(4):
            for c in out_copies(block * 4 + k):
                c.start()

    alphas = [1.0 + jax.nn.softplus(ev[i]) for i in range(K_REGIMES)]
    total = (alphas[0] + alphas[1]) + (alphas[2] + alphas[3])
    picked = jnp.zeros_like(total)
    for i in range(K_REGIMES):
        picked = jnp.where(label[...] == i, alphas[i], picked)
    loss[...] = jnp.where(mask[...] == 1, jnp.log(total) - jnp.log(picked), 0.0)
    for group in range(ROWS // 8):
        for h in range(2):
            sent = stage[h].at[pl.ds(group * 8, 8), :, pl.ds(0, LEV), :]
            pltpu.make_async_copy(sent, sent, osem.at[h, group]).wait()


def finish_call(base, halos, local, land, mask, label, bh, bo, tracers, stream, ws):
    w_in, w_hid, w_out = ws
    smem = pl.BlockSpec(memory_space=pltpu.SMEM)
    vmem = pl.BlockSpec(memory_space=pltpu.VMEM)
    anyw = pl.BlockSpec(memory_space=pl.ANY)
    return pl.pallas_call(
        finish_kernel,
        name="finish",
        out_shape=(
            jax.ShapeDtypeStruct(tracers.shape, F32),
            jax.ShapeDtypeStruct((ROWS, COLS), F32),
        ),
        in_specs=[smem] + [vmem] * 10 + [anyw] * 5,
        out_specs=(anyw, vmem),
        scratch_shapes=[pltpu.VMEM((CELLS + SPARE, COLS), F32)] * 4
        + [
            pltpu.VMEM((5, CELLS, COLS), F32),
            pltpu.VMEM((6 * SIDE, COLS), F32),
            pltpu.VMEM((CAP + WINDOW, 256), BF16),
            pltpu.VMEM((256, CAP + 256), BF16),
            pltpu.VMEM(w_in.shape, BF16),
            pltpu.VMEM(w_hid.shape, BF16),
            pltpu.VMEM(w_out.shape, BF16),
            pltpu.VMEM((256, 512), BF16),
            pltpu.VMEM((256, 512), BF16),
            pltpu.VMEM((8, 256), F32),
            pltpu.VMEM((K_REGIMES, ROWS, COLS), F32),
            pltpu.SemaphoreType.DMA((3,)),
            pltpu.SemaphoreType.DMA((3, ROWS // 8)),
            pltpu.SemaphoreType.DMA((2, ROWS // 8)),
        ],
        compiler_params=pltpu.CompilerParams(vmem_limit_bytes=VMEM_LIMIT),
    )(base, *halos, local, land, mask, label, bh, bo, tracers, stream, w_in, w_hid, w_out)


def body(tracers, stream, land_mask, convect_mask, regime_label, w_in, w_hid, b_hid, w_out, b_out):
    left, right, top, bottom, local, base = edges_call(tracers, stream, convect_mask)
    ny, nx = lax.axis_size("fy"), lax.axis_size("fx")

    def move(v, dj, di):
        pairs = [
            (b * ny + a, (b + di) * ny + a + dj)
            for a in range(ny)
            for b in range(nx)
            if 0 <= a + dj < ny and 0 <= b + di < nx
        ]
        return lax.ppermute(v, ("fx", "fy"), pairs)

    h_left, h_right = move(right, 0, 1), move(left, 0, -1)

    def with_corners(rows, r):
        at = 4 * r
        sides = [h[p * 256 + at : p * 256 + at + 16] for h in (h_left, h_right) for p in range(3)]
        return jnp.concatenate([rows] + sides, axis=0)

    h_top = move(with_corners(bottom, ROWS - 4), 1, 0)
    h_bottom = move(with_corners(top, 0), -1, 0)
    return finish_call(
        base,
        (h_left, h_right, h_top, h_bottom),
        local,
        land_mask,
        convect_mask,
        regime_label,
        b_hid,
        b_out.reshape(1, -1),
        tracers,
        stream,
        (w_in.T, w_hid, w_out),
    )


def solution(mesh):
    placed = (
        P(None, None, "fy", "fx"),
        P(None, "fy", "fx"),
        P("fy", "fx"),
        P("fy", "fx"),
        P("fy", "fx"),
        P(),
        P(),
        P(),
        P(),
        P(),
    )
    return jax.shard_map(
        body,
        mesh=mesh,
        in_specs=placed,
        out_specs=(P(None, None, "fy", "fx"), P("fy", "fx")),
        check_vma=False,
    )
```

```python
import jax
import jax.numpy as jnp
from jax import lax
from jax.experimental import pallas as pl
from jax.experimental.pallas import tpu as pltpu
from jax.sharding import PartitionSpec as P

F32, BF16, I32 = jnp.float32, jnp.bfloat16, jnp.int32
SUBSTEPS = 4
NV, LEV = 4, 60
ROWS, COLS = 64, 128
SLOTS = NV * 64
HALO_ROWS = SLOTS + 64
EXT = ROWS + 8
STRIDE = COLS + 16
CELLS = EXT * STRIDE
SPARE = COLS
SIDE = EXT * 4 + 16
NT = (((1,), (1,)), ((), ()))
TILE = 1024
CAP = 4096
WINDOW = COLS + 16
K_REGIMES = 4
VMEM_LIMIT = 61 << 20


def iota(shape, dim):
    return lax.broadcasted_iota(I32, shape, dim)


def ones_where(cond):
    return jnp.where(cond, 1.0, 0.0).astype(BF16)


def rows_kernel(x_hbm, s_hbm, top, bottom, xv, sv, sem):
    def copies(k):
        r = k if k < 4 else ROWS - 8 + k
        return (
            pltpu.make_async_copy(x_hbm.at[:, :, r, :], xv.at[k, :, pl.ds(0, LEV), :], sem.at[k]),
            pltpu.make_async_copy(s_hbm.at[:, r, :], sv.at[k, pl.ds(0, LEV), :], sem.at[8 + k]),
        )

    for k in range(8):
        for c in copies(k):
            c.start()
    for k in range(8):
        for c in copies(k):
            c.wait()
        ref, r = (top, k) if k < 4 else (bottom, k - 4)
        for f in range(NV):
            ref[pl.ds(r * HALO_ROWS + f * 64, 64), :] = xv[k, f].astype(BF16)
        ref[pl.ds(r * HALO_ROWS + SLOTS, 64), :] = sv[k].astype(BF16)


def rows_call(tracers, stream):
    row = jax.ShapeDtypeStruct((4 * HALO_ROWS, COLS), BF16)
    vmem, anyw = pl.BlockSpec(memory_space=pltpu.VMEM), pl.BlockSpec(memory_space=pl.ANY)
    return pl.pallas_call(
        rows_kernel,
        name="rows",
        out_shape=(row, row),
        in_specs=[anyw, anyw],
        out_specs=(vmem, vmem),
        scratch_shapes=[
            pltpu.VMEM((8, NV, 64, COLS), F32),
            pltpu.VMEM((8, 64, COLS), F32),
            pltpu.SemaphoreType.DMA((16,)),
        ],
        compiler_params=pltpu.CompilerParams(vmem_limit_bytes=VMEM_LIMIT),
    )(tracers, stream)


def turn_kernel(x_hbm, s_hbm, m_ref, x0, x1, flow, left, right, local, base, xv, sv, t0, t1, tf, sem, osem):
    turned, outs = (t0, t1, tf), (x0, x1, flow)

    def row_copy(i, r):
        if i == 2:
            src, dst = s_hbm.at[:, r, :], sv.at[r, pl.ds(0, LEV), :]
        else:
            src, dst = x_hbm.at[pl.ds(2 * i, 2), :, r, :], xv.at[i, r, :, pl.ds(0, LEV), :]
        return pltpu.make_async_copy(src, dst, sem.at[i, r // 8])

    @pl.loop(0, ROWS)
    def _(r):
        for i in range(3):
            row_copy(i, r).start()

    mask = m_ref[...]
    m = mask.astype(F32).astype(BF16)
    before = ones_where(iota((COLS, COLS), 0) < iota((COLS, COLS), 1))
    inside = jnp.dot(m, before, preferred_element_type=F32).astype(I32)
    local[...] = jnp.where(mask == 1, inside, -(1 << 20))
    counts = lax.dot_general(jnp.ones((8, COLS), BF16), m, NT, preferred_element_type=F32)
    base[...] = jnp.dot(
        counts.astype(BF16), before[:ROWS, :], preferred_element_type=F32
    ).astype(I32)

    def out_copy(i, group):
        rows = pl.ds(group * 8 * COLS + 8, 8 * COLS)
        dst = outs[i].at[pl.ds(group * 8 * COLS, 8 * COLS)]
        return pltpu.make_async_copy(turned[i].at[rows], dst, osem.at[i, group])

    low = iota((8, COLS), 0) < 4

    @pl.loop(0, ROWS // 8)
    def _(group):
        rows = pl.ds(group * 8, 8)
        for i in range(2):
            x = xv.at[i, rows, :, pl.ds(0, LEV), :]
            pltpu.make_async_copy(x, x, sem.at[i, group]).wait()
        v = sv.at[rows, pl.ds(0, LEV), :]
        pltpu.make_async_copy(v, v, sem.at[2, group]).wait()
        for k in range(8):
            r = group * 8 + k
            at = pl.ds(pl.multiple_of(r * COLS + 8, 8), COLS)
            for i in range(2):
                turned[i][at, :] = jnp.transpose(xv[i, r].reshape(128, COLS))
            v = 0.25 * sv[r]
            turned[2][at, :] = jnp.transpose(jnp.concatenate([v, v], axis=0))
        for i in range(3):
            out_copy(i, group).start()
        for i in range(3):
            for half in range(2):
                for ref, first, second in ((left, 0, -4), (right, COLS - 4, COLS - 8)):
                    tiles = []
                    for pair in range(2):
                        r = group * 8 + half * 4 + pair * 2
                        a = turned[i][pl.ds(r * COLS + 8 + first, 8), :]
                        b = turned[i][pl.ds((r + 1) * COLS + 8 + second, 8), :]
                        tiles.append(jnp.where(low, a, b))
                    at = pl.multiple_of(i * 256 + group * 32 + half * 16, 16)
                    ref[pl.ds(at, 16), :] = jnp.concatenate(tiles, axis=0).astype(BF16)

    for i in range(3):
        for group in range(ROWS // 8):
            out_copy(i, group).wait()


def turn_call(tracers, stream, mask):
    vmem, anyw = pl.BlockSpec(memory_space=pltpu.VMEM), pl.BlockSpec(memory_space=pl.ANY)
    cells = jax.ShapeDtypeStruct((ROWS * COLS, 128), F32)
    side = jax.ShapeDtypeStruct((3 * 256, COLS), BF16)
    return pl.pallas_call(
        turn_kernel,
        name="turn",
        out_shape=(cells, cells, cells, side, side)
        + (jax.ShapeDtypeStruct((ROWS, COLS), I32), jax.ShapeDtypeStruct((8, COLS), I32)),
        in_specs=[anyw, anyw, vmem],
        out_specs=[anyw] * 3 + [vmem] * 4,
        scratch_shapes=[
            pltpu.VMEM((2, ROWS, 2, 64, COLS), F32),
            pltpu.VMEM((ROWS, 64, COLS), F32),
        ]
        + [pltpu.VMEM((ROWS * COLS + 16, 128), F32)] * 3
        + [pltpu.SemaphoreType.DMA((3, ROWS // 8))] * 2,
        compiler_params=pltpu.CompilerParams(vmem_limit_bytes=VMEM_LIMIT),
        cost_estimate=pl.CostEstimate(flops=0, bytes_accessed=30_000_000, transcendentals=0),
    )(tracers, stream, mask)


def sides_kernel(h_top, h_bottom, left, right, left_all, right_all, tv):
    low = iota((8, COLS), 0) < 4
    for part in range(3):
        for ref, full in ((left, left_all), (right, right_all)):
            full[pl.ds(part * 288 + 16, 256), :] = ref[pl.ds(part * 256, 256), :]
    for ref, at in ((h_top, 0), (h_bottom, 272)):
        for part in range(3):
            for r in range(4):
                rows = pl.ds(r * HALO_ROWS + part * 128, 128 if part < 2 else 64)
                v = ref[rows, :].astype(F32)
                if part == 2:
                    v = 0.25 * jnp.concatenate([v, v], axis=0)
                tv[pl.ds(r * COLS + 8, COLS), :] = jnp.transpose(v)
            for full, first, second in ((left_all, 0, -4), (right_all, COLS - 4, COLS - 8)):
                tiles = []
                for pair in range(2):
                    a = tv[pl.ds(2 * pair * COLS + 8 + first, 8), :]
                    b = tv[pl.ds((2 * pair + 1) * COLS + 8 + second, 8), :]
                    tiles.append(jnp.where(low, a, b))
                full[pl.ds(part * 288 + at, 16), :] = jnp.concatenate(tiles, axis=0).astype(BF16)


def sides_call(h_top, h_bottom, left, right):
    vmem = pl.BlockSpec(memory_space=pltpu.VMEM)
    full = jax.ShapeDtypeStruct((3 * 288, COLS), BF16)
    return pl.pallas_call(
        sides_kernel,
        name="sides",
        out_shape=(full, full),
        in_specs=[vmem] * 4,
        out_specs=(vmem, vmem),
        scratch_shapes=[pltpu.VMEM((4 * COLS + 16, 128), F32)],
        compiler_params=pltpu.CompilerParams(vmem_limit_bytes=VMEM_LIMIT),
    )(h_top, h_bottom, left, right)


def leaky(v):
    return jnp.maximum(v, 0.15 * v).astype(BF16)


def finish_kernel(
    base,
    h_left,
    h_right,
    h_top,
    h_bottom,
    local,
    land,
    mask,
    label,
    bh_ref,
    bo_ref,
    x0_hbm,
    x1_hbm,
    flow_hbm,
    w_in_hbm,
    w_hid_hbm,
    w_out_hbm,
    out_hbm,
    loss,
    a0,
    a1,
    b0,
    b1,
    coef,
    side,
    packed,
    result,
    w_in,
    w_hid,
    w_out,
    w_in_p,
    w_out_p,
    bo_pad,
    ev,
    sem,
    rsem,
    osem,
):
    field = ((a0, a1), (b0, b1))
    stage = [b.reshape((CELLS + SPARE) // 128, 2, 64, COLS) for b in (b0, b1)]

    def load(src, ref, offset, i):
        grid = ref.at[pl.ds(offset, CELLS)].reshape(EXT, STRIDE, COLS)
        return pltpu.make_async_copy(src, grid.at[pl.ds(4, ROWS), pl.ds(8, COLS)], rsem.at[i])

    flow_load = load(flow_hbm, b0, 8, 2)
    field_loads = [load(x0_hbm, a0, 0, 0), load(x1_hbm, a1, 0, 1)]
    for c in [flow_load] + field_loads:
        c.start()

    weights = [
        pltpu.make_async_copy(w_in_hbm, w_in, sem.at[0]),
        pltpu.make_async_copy(w_hid_hbm, w_hid, sem.at[1]),
        pltpu.make_async_copy(w_out_hbm, w_out, sem.at[2]),
    ]
    for c in weights:
        c.start()

    first_row = lax.axis_index("fy") == 0
    last_row = lax.axis_index("fy") == lax.axis_size("fy") - 1
    first_col = lax.axis_index("fx") == 0
    last_col = lax.axis_index("fx") == lax.axis_size("fx") - 1

    packed[...] = jnp.zeros_like(packed)

    def cells_of(r):
        return pl.ds(pl.multiple_of(r * STRIDE + 8, 8), COLS)

    for part in range(3):
        for i, ref in enumerate((h_left, h_right)):
            side[pl.ds((part * 2 + i) * SIDE + 8, 288), :] = ref[
                pl.ds(part * 288, 288), :
            ].astype(F32)

    def beside(part, ref, offset):
        @pl.loop(0, EXT // 8)
        def _(group):
            for k in range(8):
                r = group * 8 + k
                at = pl.multiple_of(r * STRIDE + offset, 8)
                ref[pl.ds(at, 8), :] = side[pl.ds(part * 2 * SIDE + 4 + r * 4, 8), :]
                ref[pl.ds(at + 8 + COLS, 8), :] = side[
                    pl.ds((part * 2 + 1) * SIDE + 8 + r * 4, 8), :
                ]

    for ref, r0 in ((h_top, 0), (h_bottom, EXT - 4)):
        for r in range(4):
            v = 0.25 * ref[pl.ds(r * HALO_ROWS + SLOTS, 64), :].astype(F32)
            b0[pl.ds((r0 + r) * STRIDE + 16, COLS), :] = jnp.transpose(
                jnp.concatenate([v, v], axis=0)
            )

    beside(2, b0, 8)
    flow_load.wait()

    @pl.loop(0, 2)
    def _(block):
        @pl.loop(0, STRIDE // 8)
        def _(tile):
            q0 = pl.multiple_of((block * 35 + 1) * STRIDE + tile * 8, 8)

            def row(t):
                here = q0 + (t * STRIDE + 8)
                w, c, e = (b0[pl.ds(here + i, 8), :] for i in (-1, 0, 1))
                return w, c, e, e - w

            up, here = row(-1), row(0)
            for t in range(35):
                down = row(t + 1)
                diff = up[1] - down[1]
                w = jnp.maximum(diff + (up[0] - down[0]), 0.0)
                e = jnp.maximum((down[2] - up[2]) - diff, 0.0)
                n = jnp.maximum(up[3] + here[3], 0.0)
                s = jnp.maximum(-(here[3] + down[3]), 0.0)
                stay = 1.0 - ((w + e) + (n + s))
                for j, v in enumerate((w, e, n, s, stay)):
                    coef[j, pl.ds(q0 + t * STRIDE, 8), :] = v
                up, here = here, down

    def close_rows(r0):
        for j in range(5):
            coef[j, pl.ds(r0 * STRIDE, 3 * STRIDE), :] = jnp.zeros((3 * STRIDE, COLS), F32)

    def close_cols(offset):
        @pl.loop(1, EXT - 1)
        def _(r):
            for j in range(5):
                coef[j, pl.ds(pl.multiple_of(r * STRIDE + offset, 8), 8), :] = jnp.zeros(
                    (8, COLS), F32
                )

    pl.when(first_row)(lambda: close_rows(1))
    pl.when(last_row)(lambda: close_rows(EXT - 4))
    pl.when(first_col)(lambda: close_cols(0))
    pl.when(last_col)(lambda: close_cols(8 + COLS))

    for ref, r0 in ((h_top, 0), (h_bottom, EXT - 4)):
        for r in range(4):
            for h in range(2):
                x = ref[pl.ds(r * HALO_ROWS + h * 128, 128), :].astype(F32)
                field[0][h][pl.ds((r0 + r) * STRIDE + 8, COLS), :] = jnp.transpose(x)

    for h in range(2):
        beside(h, field[0][h], 0)
    for c in field_loads:
        c.wait()

    for step in range(SUBSTEPS):
        src, dst = field[step & 1], field[1 - (step & 1)]
        span = (EXT - 2 - 2 * step) // 2
        skip = 1 if step == SUBSTEPS - 1 else 0

        @pl.loop(0, 2)
        def _(block):
            @pl.loop(skip, STRIDE // 8 - skip)
            def _(tile):
                q0 = pl.multiple_of((block * span + step + 1) * STRIDE + tile * 8, 8)

                def at(h, t, offset=0):
                    return src[h][pl.ds(q0 + (t * STRIDE + offset), 8), :]

                up = [at(h, -1) for h in range(2)]
                cell = [at(h, 0) for h in range(2)]
                for t in range(span):
                    q = q0 + t * STRIDE
                    w, e, n, s, stay = (coef[j, pl.ds(q, 8), :] for j in range(5))
                    for h in range(2):
                        down = at(h, t + 1)
                        own = stay * cell[h] + w * at(h, t, -1)
                        ahead = e * at(h, t, 1) + n * up[h]
                        dst[h][pl.ds(q, 8), :] = (own + ahead) + s * down
                        up[h], cell[h] = cell[h], down

    for c in weights:
        c.wait()
    slot_id, source = iota((256, 256), 0), iota((256, 256), 1)
    level = slot_id & 63
    wanted = jnp.where(level < LEV, (slot_id >> 6) * LEV + level, -1)
    for_in = jnp.where(slot_id == LEV, NV * LEV, wanted)
    for_out = jnp.where(
        jnp.logical_and(slot_id >= LEV, slot_id < 64), NV * LEV + slot_id - LEV, wanted
    )
    pick_in, pick_out = ones_where(for_in == source), ones_where(for_out == source)
    n_in, n_out = w_in.shape[0], w_out.shape[0]
    w_in_p[...] = jnp.dot(pick_in[:, :n_in], w_in[...], preferred_element_type=F32).astype(BF16)
    w_out_p[...] = jnp.dot(pick_out[:, :n_out], w_out[...], preferred_element_type=F32).astype(BF16)
    bo_pad[...] = jnp.zeros_like(bo_pad)
    bo_pad[0:1, 0:n_out] = bo_ref[...]
    out_row = jnp.broadcast_to(bo_pad[0:1, :], (256, 256))
    out_bias = jnp.sum(jnp.where(for_out == source, out_row, 0.0), axis=1, keepdims=True)

    real = (iota((COLS, 256), 1) & 63) < LEV
    land_slot = jnp.where(iota((COLS, 256), 1) == LEV, 4.0, 0.0).astype(BF16)
    window_spot = iota((WINDOW, COLS), 0)
    spot = iota((256, COLS), 0)

    @pl.loop(0, ROWS // 2)
    def _(pair):
        moved = []
        for k in range(2):
            r = pair * 2 + k
            x = jnp.concatenate(
                [field[0][h][cells_of(r + 4), :] for h in range(2)], axis=1
            )
            x = jnp.where(real, x, 0.0).astype(BF16)
            hit = window_spot == local[pl.ds(r, 1), :] + (base[0, r] & 15)
            land_hit = jnp.logical_and(hit, land[pl.ds(r, 1), :] == 1)
            hot = jnp.concatenate([ones_where(hit), ones_where(land_hit)], axis=1)
            moved.append(
                jnp.dot(
                    hot, jnp.concatenate([x, land_slot], axis=0), preferred_element_type=F32
                ).astype(BF16)
            )
        for k in range(2):
            r = pair * 2 + k
            packed[pl.ds(pl.multiple_of((base[0, r] >> 4) * 16, 16), WINDOW), :] += moved[k]

    tiles = (base[0, ROWS] + TILE - 1) // TILE

    @pl.loop(0, tiles)
    def _(i):
        half = TILE // 2
        hs = []
        for c in range(2):
            at = pl.ds(pl.multiple_of(i * TILE + c * half, half), half)
            hs.append(
                leaky(
                    jnp.dot(packed[at, :], w_in_p[...], preferred_element_type=F32)
                    + bh_ref[0:1, :]
                )
            )
        for layer in range(6):
            for c in range(2):
                hs[c] = leaky(
                    lax.dot_general(hs[c], w_hid[layer], NT, preferred_element_type=F32)
                    + bh_ref[layer + 1 : layer + 2, :]
                )
        for c in range(2):
            at = pl.ds(pl.multiple_of(i * TILE + c * half, half), half)
            result[:, at] = (
                lax.dot_general(w_out_p[...], hs[c], NT, preferred_element_type=F32) + out_bias
            ).astype(BF16)

    result[:, pl.ds(pl.multiple_of(tiles * TILE, TILE), 256)] = jnp.zeros((256, 256), BF16)

    def out_copies(r):
        return [
            pltpu.make_async_copy(
                stage[h].at[r, :, pl.ds(0, LEV), :],
                out_hbm.at[pl.ds(2 * h, 2), :, r, :],
                osem.at[h, r // 8],
            )
            for h in range(2)
        ]

    @pl.loop(0, ROWS // 4)
    def _(block):
        for k in range(4):
            r = block * 4 + k
            hot = ones_where(spot == local[pl.ds(r, 1), :] + (base[0, r] & 127))
            at = pl.ds(pl.multiple_of((base[0, r] >> 7) * 128, 128), 256)
            back = jnp.dot(result[:, at], hot, preferred_element_type=F32)
            for i in range(K_REGIMES):
                ev[i, pl.ds(r, 1), :] = back[LEV + i : LEV + i + 1, :]
            for h in range(2):
                new = jnp.transpose(field[0][h][cells_of(r + 4), :]) + back[h * 128 : h * 128 + 128]
                stage[h][r] = new.reshape(2, 64, COLS)
        for k in range(4):
            for c in out_copies(block * 4 + k):
                c.start()

    alphas = [1.0 + jax.nn.softplus(ev[i]) for i in range(K_REGIMES)]
    total = (alphas[0] + alphas[1]) + (alphas[2] + alphas[3])
    picked = jnp.zeros_like(total)
    for i in range(K_REGIMES):
        picked = jnp.where(label[...] == i, alphas[i], picked)
    loss[...] = jnp.where(mask[...] == 1, jnp.log(total) - jnp.log(picked), 0.0)
    for group in range(ROWS // 8):
        for h in range(2):
            sent = stage[h].at[pl.ds(group * 8, 8), :, pl.ds(0, LEV), :]
            pltpu.make_async_copy(sent, sent, osem.at[h, group]).wait()


def finish_call(base, halos, local, land, mask, label, bh, bo, turned, ws):
    w_in, w_hid, w_out = ws
    smem = pl.BlockSpec(memory_space=pltpu.SMEM)
    vmem = pl.BlockSpec(memory_space=pltpu.VMEM)
    anyw = pl.BlockSpec(memory_space=pl.ANY)
    return pl.pallas_call(
        finish_kernel,
        name="finish",
        out_shape=(
            jax.ShapeDtypeStruct((NV, LEV, ROWS, COLS), F32),
            jax.ShapeDtypeStruct((ROWS, COLS), F32),
        ),
        in_specs=[smem] + [vmem] * 10 + [anyw] * 6,
        out_specs=(anyw, vmem),
        scratch_shapes=[pltpu.VMEM((CELLS + SPARE, COLS), F32)] * 4
        + [
            pltpu.VMEM((5, CELLS, COLS), F32),
            pltpu.VMEM((6 * SIDE, COLS), F32),
            pltpu.VMEM((CAP + WINDOW, 256), BF16),
            pltpu.VMEM((256, CAP + 256), BF16),
            pltpu.VMEM(w_in.shape, BF16),
            pltpu.VMEM(w_hid.shape, BF16),
            pltpu.VMEM(w_out.shape, BF16),
            pltpu.VMEM((256, 512), BF16),
            pltpu.VMEM((256, 512), BF16),
            pltpu.VMEM((8, 256), F32),
            pltpu.VMEM((K_REGIMES, ROWS, COLS), F32),
            pltpu.SemaphoreType.DMA((3,)),
            pltpu.SemaphoreType.DMA((3,)),
            pltpu.SemaphoreType.DMA((2, ROWS // 8)),
        ],
        compiler_params=pltpu.CompilerParams(vmem_limit_bytes=VMEM_LIMIT),
    )(base, *halos, local, land, mask, label, bh, bo, *turned, w_in, w_hid, w_out)


def body(tracers, stream, land_mask, convect_mask, regime_label, w_in, w_hid, b_hid, w_out, b_out):
    top, bottom = rows_call(tracers, stream)
    ny, nx = lax.axis_size("fy"), lax.axis_size("fx")

    def move(v, dj, di):
        pairs = [
            (b * ny + a, (b + di) * ny + a + dj)
            for a in range(ny)
            for b in range(nx)
            if 0 <= a + dj < ny and 0 <= b + di < nx
        ]
        return lax.ppermute(v, ("fx", "fy"), pairs)

    h_top, h_bottom = move(bottom, 1, 0), move(top, -1, 0)
    x0, x1, flow, left, right, local, base = turn_call(tracers, stream, convect_mask)
    left, right = sides_call(h_top, h_bottom, left, right)
    h_left, h_right = move(right, 0, 1), move(left, 0, -1)
    return finish_call(
        base,
        (h_left, h_right, h_top, h_bottom),
        local,
        land_mask,
        convect_mask,
        regime_label,
        b_hid,
        b_out.reshape(1, -1),
        tuple(v.reshape(ROWS, COLS, 128) for v in (x0, x1, flow)),
        (w_in.T, w_hid, w_out),
    )


def solution(mesh):
    placed = (
        P(None, None, "fy", "fx"),
        P(None, "fy", "fx"),
        P("fy", "fx"),
        P("fy", "fx"),
        P("fy", "fx"),
        P(),
        P(),
        P(),
        P(),
        P(),
    )
    return jax.shard_map(
        body,
        mesh=mesh,
        in_specs=placed,
        out_specs=(P(None, None, "fy", "fx"), P("fy", "fx")),
        check_vma=False,
    )
```

```python
import jax
import jax.numpy as jnp
from jax import lax
from jax.experimental import pallas as pl
from jax.experimental.pallas import tpu as pltpu
from jax.sharding import PartitionSpec as P

F32, BF16, I32 = jnp.float32, jnp.bfloat16, jnp.int32
SUBSTEPS = 4
NV, LEV = 4, 60
ROWS, COLS = 64, 128
SLOTS = NV * 64
HALO_ROWS = SLOTS + 64
EXT = ROWS + 8
STRIDE = COLS + 16
CELLS = EXT * STRIDE
SPARE = COLS
SIDE = EXT * 4 + 16
NT = (((1,), (1,)), ((), ()))
TILE = 1024
CAP = 4096
WINDOW = COLS + 16
K_REGIMES = 4
VMEM_LIMIT = 61 << 20


def iota(shape, dim):
    return lax.broadcasted_iota(I32, shape, dim)


def ones_where(cond):
    return jnp.where(cond, 1.0, 0.0).astype(BF16)


def rows_kernel(x_hbm, s_hbm, top, bottom, xv, sv, sem):
    def copies(k):
        r = k if k < 4 else ROWS - 8 + k
        return (
            pltpu.make_async_copy(x_hbm.at[:, :, r, :], xv.at[k, :, pl.ds(0, LEV), :], sem.at[k]),
            pltpu.make_async_copy(s_hbm.at[:, r, :], sv.at[k, pl.ds(0, LEV), :], sem.at[8 + k]),
        )

    for k in range(8):
        for c in copies(k):
            c.start()
    for k in range(8):
        for c in copies(k):
            c.wait()
        ref, r = (top, k) if k < 4 else (bottom, k - 4)
        for f in range(NV):
            ref[pl.ds(r * HALO_ROWS + f * 64, 64), :] = xv[k, f].astype(BF16)
        ref[pl.ds(r * HALO_ROWS + SLOTS, 64), :] = sv[k].astype(BF16)


def rows_call(tracers, stream):
    row = jax.ShapeDtypeStruct((4 * HALO_ROWS, COLS), BF16)
    vmem, anyw = pl.BlockSpec(memory_space=pltpu.VMEM), pl.BlockSpec(memory_space=pl.ANY)
    return pl.pallas_call(
        rows_kernel,
        name="rows",
        out_shape=(row, row),
        in_specs=[anyw, anyw],
        out_specs=(vmem, vmem),
        scratch_shapes=[
            pltpu.VMEM((8, NV, 64, COLS), F32),
            pltpu.VMEM((8, 64, COLS), F32),
            pltpu.SemaphoreType.DMA((16,)),
        ],
        compiler_params=pltpu.CompilerParams(vmem_limit_bytes=VMEM_LIMIT),
    )(tracers, stream)


def turn_kernel(x_hbm, s_hbm, m_ref, x0, x1, flow, left, right, local, base, xv, sv, t0, t1, tf, sem, osem):
    turned, outs = (t0, t1, tf), (x0, x1, flow)

    def row_copy(i, r):
        if i == 1:
            src, dst = s_hbm.at[:, r, :], sv.at[r, pl.ds(0, LEV), :]
        else:
            src, dst = x_hbm.at[:, :, r, :], xv.at[r, :, pl.ds(0, LEV), :]
        return pltpu.make_async_copy(src, dst, sem.at[i, r // 8])

    @pl.loop(0, ROWS)
    def _(r):
        for i in range(2):
            row_copy(i, r).start()

    mask = m_ref[...]
    m = mask.astype(F32).astype(BF16)
    before = ones_where(iota((COLS, COLS), 0) < iota((COLS, COLS), 1))
    inside = jnp.dot(m, before, preferred_element_type=F32).astype(I32)
    local[...] = jnp.where(mask == 1, inside, -(1 << 20))
    counts = lax.dot_general(jnp.ones((8, COLS), BF16), m, NT, preferred_element_type=F32)
    base[...] = jnp.dot(
        counts.astype(BF16), before[:ROWS, :], preferred_element_type=F32
    ).astype(I32)

    def out_copy(i, group):
        rows = pl.ds(group * 8 * COLS + 8, 8 * COLS)
        dst = outs[i].at[pl.ds(group * 8 * COLS, 8 * COLS)]
        return pltpu.make_async_copy(turned[i].at[rows], dst, osem.at[i, group])

    low = iota((8, COLS), 0) < 4

    @pl.loop(0, ROWS // 8)
    def _(group):
        rows = pl.ds(group * 8, 8)
        x = xv.at[rows, :, pl.ds(0, LEV), :]
        pltpu.make_async_copy(x, x, sem.at[0, group]).wait()
        v = sv.at[rows, pl.ds(0, LEV), :]
        pltpu.make_async_copy(v, v, sem.at[1, group]).wait()
        for k in range(8):
            r = group * 8 + k
            at = pl.ds(pl.multiple_of(r * COLS + 8, 8), COLS)
            for i in range(2):
                turned[i][at, :] = jnp.transpose(xv[r, pl.ds(2 * i, 2)].reshape(128, COLS))
            v = 0.25 * sv[r]
            turned[2][at, :] = jnp.transpose(jnp.concatenate([v, v], axis=0))
        for i in range(3):
            out_copy(i, group).start()
        for i in range(3):
            for half in range(2):
                for ref, first, second in ((left, 0, -4), (right, COLS - 4, COLS - 8)):
                    tiles = []
                    for pair in range(2):
                        r = group * 8 + half * 4 + pair * 2
                        a = turned[i][pl.ds(r * COLS + 8 + first, 8), :]
                        b = turned[i][pl.ds((r + 1) * COLS + 8 + second, 8), :]
                        tiles.append(jnp.where(low, a, b))
                    at = pl.multiple_of(i * 256 + group * 32 + half * 16, 16)
                    ref[pl.ds(at, 16), :] = jnp.concatenate(tiles, axis=0).astype(BF16)

    for i in range(3):
        for group in range(ROWS // 8):
            out_copy(i, group).wait()


def turn_call(tracers, stream, mask):
    vmem, anyw = pl.BlockSpec(memory_space=pltpu.VMEM), pl.BlockSpec(memory_space=pl.ANY)
    cells = jax.ShapeDtypeStruct((ROWS * COLS, 128), F32)
    side = jax.ShapeDtypeStruct((3 * 256, COLS), BF16)
    return pl.pallas_call(
        turn_kernel,
        name="turn",
        out_shape=(cells, cells, cells, side, side)
        + (jax.ShapeDtypeStruct((ROWS, COLS), I32), jax.ShapeDtypeStruct((8, COLS), I32)),
        in_specs=[anyw, anyw, vmem],
        out_specs=[anyw] * 3 + [vmem] * 4,
        scratch_shapes=[
            pltpu.VMEM((ROWS, NV, 64, COLS), F32),
            pltpu.VMEM((ROWS, 64, COLS), F32),
        ]
        + [pltpu.VMEM((ROWS * COLS + 16, 128), F32)] * 3
        + [pltpu.SemaphoreType.DMA((3, ROWS // 8))] * 2,
        compiler_params=pltpu.CompilerParams(vmem_limit_bytes=VMEM_LIMIT),
        cost_estimate=pl.CostEstimate(flops=0, bytes_accessed=30_000_000, transcendentals=0),
    )(tracers, stream, mask)


def sides_kernel(h_top, h_bottom, left, right, left_all, right_all, tv):
    low = iota((8, COLS), 0) < 4
    for part in range(3):
        for ref, full in ((left, left_all), (right, right_all)):
            full[pl.ds(part * 288 + 16, 256), :] = ref[pl.ds(part * 256, 256), :]
    for ref, at in ((h_top, 0), (h_bottom, 272)):
        for part in range(3):
            for r in range(4):
                rows = pl.ds(r * HALO_ROWS + part * 128, 128 if part < 2 else 64)
                v = ref[rows, :].astype(F32)
                if part == 2:
                    v = 0.25 * jnp.concatenate([v, v], axis=0)
                tv[pl.ds(r * COLS + 8, COLS), :] = jnp.transpose(v)
            for full, first, second in ((left_all, 0, -4), (right_all, COLS - 4, COLS - 8)):
                tiles = []
                for pair in range(2):
                    a = tv[pl.ds(2 * pair * COLS + 8 + first, 8), :]
                    b = tv[pl.ds((2 * pair + 1) * COLS + 8 + second, 8), :]
                    tiles.append(jnp.where(low, a, b))
                full[pl.ds(part * 288 + at, 16), :] = jnp.concatenate(tiles, axis=0).astype(BF16)


def sides_call(h_top, h_bottom, left, right):
    vmem = pl.BlockSpec(memory_space=pltpu.VMEM)
    full = jax.ShapeDtypeStruct((3 * 288, COLS), BF16)
    return pl.pallas_call(
        sides_kernel,
        name="sides",
        out_shape=(full, full),
        in_specs=[vmem] * 4,
        out_specs=(vmem, vmem),
        scratch_shapes=[pltpu.VMEM((4 * COLS + 16, 128), F32)],
        compiler_params=pltpu.CompilerParams(vmem_limit_bytes=VMEM_LIMIT),
    )(h_top, h_bottom, left, right)


def leaky(v):
    return jnp.maximum(v, 0.15 * v).astype(BF16)


def finish_kernel(
    base,
    h_left,
    h_right,
    h_top,
    h_bottom,
    local,
    land,
    mask,
    label,
    bh_ref,
    bo_ref,
    x0_hbm,
    x1_hbm,
    flow_hbm,
    w_in_hbm,
    w_hid_hbm,
    w_out_hbm,
    out_hbm,
    loss,
    a0,
    a1,
    b0,
    b1,
    coef,
    side,
    packed,
    result,
    w_in,
    w_hid,
    w_out,
    w_in_p,
    w_out_p,
    bo_pad,
    ev,
    sem,
    rsem,
    osem,
):
    field = ((a0, a1), (b0, b1))
    stage = [b.reshape((CELLS + SPARE) // 128, 2, 64, COLS) for b in (b0, b1)]

    def load(src, ref, offset, i):
        grid = ref.at[pl.ds(offset, CELLS)].reshape(EXT, STRIDE, COLS)
        return pltpu.make_async_copy(src, grid.at[pl.ds(4, ROWS), pl.ds(8, COLS)], rsem.at[i])

    flow_load = load(flow_hbm, b0, 8, 2)
    field_loads = [load(x0_hbm, a0, 0, 0), load(x1_hbm, a1, 0, 1)]
    for c in [flow_load] + field_loads:
        c.start()

    weights = [
        pltpu.make_async_copy(w_in_hbm, w_in, sem.at[0]),
        pltpu.make_async_copy(w_hid_hbm, w_hid, sem.at[1]),
        pltpu.make_async_copy(w_out_hbm, w_out, sem.at[2]),
    ]
    for c in weights:
        c.start()

    first_row = lax.axis_index("fy") == 0
    last_row = lax.axis_index("fy") == lax.axis_size("fy") - 1
    first_col = lax.axis_index("fx") == 0
    last_col = lax.axis_index("fx") == lax.axis_size("fx") - 1

    packed[...] = jnp.zeros_like(packed)

    def cells_of(r):
        return pl.ds(pl.multiple_of(r * STRIDE + 8, 8), COLS)

    for part in range(3):
        for i, ref in enumerate((h_left, h_right)):
            side[pl.ds((part * 2 + i) * SIDE + 8, 288), :] = ref[
                pl.ds(part * 288, 288), :
            ].astype(F32)

    def beside(part, ref, offset):
        @pl.loop(0, EXT // 8)
        def _(group):
            for k in range(8):
                r = group * 8 + k
                at = pl.multiple_of(r * STRIDE + offset, 8)
                ref[pl.ds(at, 8), :] = side[pl.ds(part * 2 * SIDE + 4 + r * 4, 8), :]
                ref[pl.ds(at + 8 + COLS, 8), :] = side[
                    pl.ds((part * 2 + 1) * SIDE + 8 + r * 4, 8), :
                ]

    for ref, r0 in ((h_top, 0), (h_bottom, EXT - 4)):
        for r in range(4):
            v = 0.25 * ref[pl.ds(r * HALO_ROWS + SLOTS, 64), :].astype(F32)
            b0[pl.ds((r0 + r) * STRIDE + 16, COLS), :] = jnp.transpose(
                jnp.concatenate([v, v], axis=0)
            )

    beside(2, b0, 8)
    flow_load.wait()

    @pl.loop(0, 2)
    def _(block):
        @pl.loop(0, STRIDE // 8)
        def _(tile):
            q0 = pl.multiple_of((block * 35 + 1) * STRIDE + tile * 8, 8)

            def row(t):
                here = q0 + (t * STRIDE + 8)
                w, c, e = (b0[pl.ds(here + i, 8), :] for i in (-1, 0, 1))
                return w, c, e, e - w

            up, here = row(-1), row(0)
            for t in range(35):
                down = row(t + 1)
                diff = up[1] - down[1]
                w = jnp.maximum(diff + (up[0] - down[0]), 0.0)
                e = jnp.maximum((down[2] - up[2]) - diff, 0.0)
                n = jnp.maximum(up[3] + here[3], 0.0)
                s = jnp.maximum(-(here[3] + down[3]), 0.0)
                stay = 1.0 - ((w + e) + (n + s))
                for j, v in enumerate((w, e, n, s, stay)):
                    coef[j, pl.ds(q0 + t * STRIDE, 8), :] = v
                up, here = here, down

    def close_rows(r0):
        for j in range(5):
            coef[j, pl.ds(r0 * STRIDE, 3 * STRIDE), :] = jnp.zeros((3 * STRIDE, COLS), F32)

    def close_cols(offset):
        @pl.loop(1, EXT - 1)
        def _(r):
            for j in range(5):
                coef[j, pl.ds(pl.multiple_of(r * STRIDE + offset, 8), 8), :] = jnp.zeros(
                    (8, COLS), F32
                )

    pl.when(first_row)(lambda: close_rows(1))
    pl.when(last_row)(lambda: close_rows(EXT - 4))
    pl.when(first_col)(lambda: close_cols(0))
    pl.when(last_col)(lambda: close_cols(8 + COLS))

    for ref, r0 in ((h_top, 0), (h_bottom, EXT - 4)):
        for r in range(4):
            for h in range(2):
                x = ref[pl.ds(r * HALO_ROWS + h * 128, 128), :].astype(F32)
                field[0][h][pl.ds((r0 + r) * STRIDE + 8, COLS), :] = jnp.transpose(x)

    for h in range(2):
        beside(h, field[0][h], 0)
    for c in field_loads:
        c.wait()

    for step in range(SUBSTEPS):
        src, dst = field[step & 1], field[1 - (step & 1)]
        span = EXT - 2 - 2 * step
        skip = 1 if step == SUBSTEPS - 1 else 0

        @pl.loop(skip, STRIDE // 8 - skip)
        def _(tile):
            q0 = pl.multiple_of((step + 1) * STRIDE + tile * 8, 8)

            def at(h, t, offset=0):
                return src[h][pl.ds(q0 + (t * STRIDE + offset), 8), :]

            up = [at(h, -1) for h in range(2)]
            cell = [at(h, 0) for h in range(2)]
            for t in range(span):
                q = q0 + t * STRIDE
                w, e, n, s, stay = (coef[j, pl.ds(q, 8), :] for j in range(5))
                for h in range(2):
                    down = at(h, t + 1)
                    own = stay * cell[h] + w * at(h, t, -1)
                    ahead = e * at(h, t, 1) + n * up[h]
                    dst[h][pl.ds(q, 8), :] = (own + ahead) + s * down
                    up[h], cell[h] = cell[h], down

    for c in weights:
        c.wait()
    slot_id, source = iota((256, 256), 0), iota((256, 256), 1)
    level = slot_id & 63
    wanted = jnp.where(level < LEV, (slot_id >> 6) * LEV + level, -1)
    for_in = jnp.where(slot_id == LEV, NV * LEV, wanted)
    for_out = jnp.where(
        jnp.logical_and(slot_id >= LEV, slot_id < 64), NV * LEV + slot_id - LEV, wanted
    )
    pick_in, pick_out = ones_where(for_in == source), ones_where(for_out == source)
    n_in, n_out = w_in.shape[0], w_out.shape[0]
    w_in_p[...] = jnp.dot(pick_in[:, :n_in], w_in[...], preferred_element_type=F32).astype(BF16)
    w_out_p[...] = jnp.dot(pick_out[:, :n_out], w_out[...], preferred_element_type=F32).astype(BF16)
    bo_pad[...] = jnp.zeros_like(bo_pad)
    bo_pad[0:1, 0:n_out] = bo_ref[...]
    out_row = jnp.broadcast_to(bo_pad[0:1, :], (256, 256))
    out_bias = jnp.sum(jnp.where(for_out == source, out_row, 0.0), axis=1, keepdims=True)

    real = (iota((COLS, 256), 1) & 63) < LEV
    land_slot = jnp.where(iota((COLS, 256), 1) == LEV, 4.0, 0.0).astype(BF16)
    window_spot = iota((WINDOW, COLS), 0)
    spot = iota((256, COLS), 0)

    @pl.loop(0, ROWS // 4)
    def _(block):
        moved = []
        for k in range(4):
            r = block * 4 + k
            x = jnp.concatenate(
                [field[0][h][cells_of(r + 4), :] for h in range(2)], axis=1
            )
            x = jnp.where(real, x, 0.0).astype(BF16)
            hit = window_spot == local[pl.ds(r, 1), :] + (base[0, r] & 15)
            land_hit = jnp.logical_and(hit, land[pl.ds(r, 1), :] == 1)
            hot = jnp.concatenate([ones_where(hit), ones_where(land_hit)], axis=1)
            moved.append(
                jnp.dot(
                    hot, jnp.concatenate([x, land_slot], axis=0), preferred_element_type=F32
                ).astype(BF16)
            )
        for k in range(4):
            r = block * 4 + k
            packed[pl.ds(pl.multiple_of((base[0, r] >> 4) * 16, 16), WINDOW), :] += moved[k]

    tiles = (base[0, ROWS] + TILE - 1) // TILE

    @pl.loop(0, tiles)
    def _(i):
        half = TILE // 2
        hs = []
        for c in range(2):
            at = pl.ds(pl.multiple_of(i * TILE + c * half, half), half)
            hs.append(
                leaky(
                    jnp.dot(packed[at, :], w_in_p[...], preferred_element_type=F32)
                    + bh_ref[0:1, :]
                )
            )
        for layer in range(6):
            for c in range(2):
                hs[c] = leaky(
                    lax.dot_general(hs[c], w_hid[layer], NT, preferred_element_type=F32)
                    + bh_ref[layer + 1 : layer + 2, :]
                )
        for c in range(2):
            at = pl.ds(pl.multiple_of(i * TILE + c * half, half), half)
            result[:, at] = (
                lax.dot_general(w_out_p[...], hs[c], NT, preferred_element_type=F32) + out_bias
            ).astype(BF16)

    result[:, pl.ds(pl.multiple_of(tiles * TILE, TILE), 256)] = jnp.zeros((256, 256), BF16)

    def out_copies(r):
        return [
            pltpu.make_async_copy(
                stage[h].at[r, :, pl.ds(0, LEV), :],
                out_hbm.at[pl.ds(2 * h, 2), :, r, :],
                osem.at[h, r // 8],
            )
            for h in range(2)
        ]

    @pl.loop(0, ROWS // 8)
    def _(block):
        for k in range(8):
            r = block * 8 + k
            hot = ones_where(spot == local[pl.ds(r, 1), :] + (base[0, r] & 127))
            at = pl.ds(pl.multiple_of((base[0, r] >> 7) * 128, 128), 256)
            back = jnp.dot(result[:, at], hot, preferred_element_type=F32)
            for i in range(K_REGIMES):
                ev[i, pl.ds(r, 1), :] = back[LEV + i : LEV + i + 1, :]
            for h in range(2):
                new = jnp.transpose(field[0][h][cells_of(r + 4), :]) + back[h * 128 : h * 128 + 128]
                stage[h][r] = new.reshape(2, 64, COLS)
        for k in range(8):
            for c in out_copies(block * 8 + k):
                c.start()

    alphas = [1.0 + jax.nn.softplus(ev[i]) for i in range(K_REGIMES)]
    total = (alphas[0] + alphas[1]) + (alphas[2] + alphas[3])
    picked = jnp.zeros_like(total)
    for i in range(K_REGIMES):
        picked = jnp.where(label[...] == i, alphas[i], picked)
    loss[...] = jnp.where(mask[...] == 1, jnp.log(total) - jnp.log(picked), 0.0)
    for group in range(ROWS // 8):
        for h in range(2):
            sent = stage[h].at[pl.ds(group * 8, 8), :, pl.ds(0, LEV), :]
            pltpu.make_async_copy(sent, sent, osem.at[h, group]).wait()


def finish_call(base, halos, local, land, mask, label, bh, bo, turned, ws):
    w_in, w_hid, w_out = ws
    smem = pl.BlockSpec(memory_space=pltpu.SMEM)
    vmem = pl.BlockSpec(memory_space=pltpu.VMEM)
    anyw = pl.BlockSpec(memory_space=pl.ANY)
    return pl.pallas_call(
        finish_kernel,
        name="finish",
        out_shape=(
            jax.ShapeDtypeStruct((NV, LEV, ROWS, COLS), F32),
            jax.ShapeDtypeStruct((ROWS, COLS), F32),
        ),
        in_specs=[smem] + [vmem] * 10 + [anyw] * 6,
        out_specs=(anyw, vmem),
        scratch_shapes=[pltpu.VMEM((CELLS + SPARE, COLS), F32)] * 4
        + [
            pltpu.VMEM((5, CELLS, COLS), F32),
            pltpu.VMEM((6 * SIDE, COLS), F32),
            pltpu.VMEM((CAP + WINDOW, 256), BF16),
            pltpu.VMEM((256, CAP + 256), BF16),
            pltpu.VMEM(w_in.shape, BF16),
            pltpu.VMEM(w_hid.shape, BF16),
            pltpu.VMEM(w_out.shape, BF16),
            pltpu.VMEM((256, 512), BF16),
            pltpu.VMEM((256, 512), BF16),
            pltpu.VMEM((8, 256), F32),
            pltpu.VMEM((K_REGIMES, ROWS, COLS), F32),
            pltpu.SemaphoreType.DMA((3,)),
            pltpu.SemaphoreType.DMA((3,)),
            pltpu.SemaphoreType.DMA((2, ROWS // 8)),
        ],
        compiler_params=pltpu.CompilerParams(vmem_limit_bytes=VMEM_LIMIT),
    )(base, *halos, local, land, mask, label, bh, bo, *turned, w_in, w_hid, w_out)


def body(tracers, stream, land_mask, convect_mask, regime_label, w_in, w_hid, b_hid, w_out, b_out):
    top, bottom = rows_call(tracers, stream)
    ny, nx = lax.axis_size("fy"), lax.axis_size("fx")

    def move(v, dj, di):
        pairs = [
            (b * ny + a, (b + di) * ny + a + dj)
            for a in range(ny)
            for b in range(nx)
            if 0 <= a + dj < ny and 0 <= b + di < nx
        ]
        return lax.ppermute(v, ("fx", "fy"), pairs)

    h_top, h_bottom = move(bottom, 1, 0), move(top, -1, 0)
    x0, x1, flow, left, right, local, base = turn_call(tracers, stream, convect_mask)
    left, right = sides_call(h_top, h_bottom, left, right)
    h_left, h_right = move(right, 0, 1), move(left, 0, -1)
    return finish_call(
        base,
        (h_left, h_right, h_top, h_bottom),
        local,
        land_mask,
        convect_mask,
        regime_label,
        b_hid,
        b_out.reshape(1, -1),
        tuple(v.reshape(ROWS, COLS, 128) for v in (x0, x1, flow)),
        (w_in.T, w_hid, w_out),
    )


def solution(mesh):
    placed = (
        P(None, None, "fy", "fx"),
        P(None, "fy", "fx"),
        P("fy", "fx"),
        P("fy", "fx"),
        P("fy", "fx"),
        P(),
        P(),
        P(),
        P(),
        P(),
    )
    return jax.shard_map(
        body,
        mesh=mesh,
        in_specs=placed,
        out_specs=(P(None, None, "fy", "fx"), P("fy", "fx")),
        check_vma=False,
    )
```
